256 devices in a mesh: gx: 8 (over z_hi, core), gy: 4 (over x), gz: 8 (over y, z_lo).
Axes of the slice: x: 4, y: 4, z: 8 (z_hi: 4, z_lo: 2; z = z_hi * 2 + z_lo), core: 2. Of those that a mesh axis runs over, the one named last changes fastest.
Arguments:
- features: float32 [16, 8, 8, 128, 128], P('gx', 'gy', 'gz'), may hold values from -6 to 6
- positions: float32 [16, 8, 8, 3, 128], P('gx', 'gy', 'gz'), may hold values from 0 to 1
- counts: int32 [16, 8, 8], P('gx', 'gy', 'gz'), may hold values from 64 to 128, as said below
- waves: int32 [3, 2048], replicated, may hold values from -8 to 8
- filter_table: float32 [2048, 128], replicated, may hold values from -6 to 6
- w_value: float32 [128, 128], replicated, may hold values from -0.5 to 0.5
- w_charge: float32 [128, 128], replicated, may hold values from -0.5 to 0.5
- radial_mix: float32 [8, 128], replicated, may hold values from -2 to 2
- w_hidden: float32 [128, 256], replicated, may hold values from -0.5 to 0.5
- w_out: float32 [256, 128], replicated, may hold values from -0.375 to 0.375
Outputs:
- updated: float32 [16, 8, 8, 128, 128], P('gx', 'gy', 'gz')
The draws below stay inside these ranges and needn't reach their ends.
Inputs may be any that keep to these rules, and one draw needn't show every extreme that they name: `counts`: slots below a cell's count hold atoms, the others are padding.
All inputs are finite; a program needn't handle non-finite values.
Results may differ from the reference program's by a relative error of at most 0.0001.
Values sent between devices are 32-bit elements; how exact they have to be, the bound alone decides.
A program may use at most 64 MiB of HBM per device.

```python
import math
import jax
import jax.numpy as jnp
from jax import lax

C = 128
K = 2048
B = 8
F = 256
A = 128
NCX = 16
NCY = 8
NCZ = 8


def draw_counts(key, part):
    cell_total = NCX * NCY * NCZ
    key_fill, key_top, key_low = jax.random.split(jax.random.fold_in(key, 11), 3)
    filled = jax.random.randint(key_fill, (cell_total,), A // 2, A + 1, dtype=jnp.int32)
    top_cell = jax.random.randint(key_top, (), 0, cell_total, dtype=jnp.int32)
    low_cell = (top_cell + 1 + jax.random.randint(key_low, (), 0, cell_total - 1, dtype=jnp.int32)) % cell_total
    cell_ids = jnp.arange(cell_total, dtype=jnp.int32)
    filled = jnp.where(cell_ids == top_cell, A, filled)
    filled = jnp.where(cell_ids == low_cell, A // 2, filled)
    return filled.reshape((NCX, NCY, NCZ))


def touch_ends(values, own_key, smallest, top_value):
    place = [jax.random.randint(jax.random.fold_in(own_key, axis), (), 0, length) for axis, length in enumerate(values.shape)]
    longest = values.shape.index(max(values.shape))
    next_to = place[:longest] + [(place[longest] + 1) % values.shape[longest]] + place[longest + 1:]
    return values.at[tuple(place)].set(smallest).at[tuple(next_to)].set(top_value)


def levels(rng, extent, shards, low, largest):
    def one(axis_at, shards_of):
        draws = jax.random.uniform(jax.random.fold_in(jax.random.fold_in(rng, 6), axis_at), (shards_of,), jnp.float32, low / len(shards), largest / len(shards))
        return jnp.repeat(jnp.exp(draws), extent[axis_at] // shards_of).reshape((-1,) + (1,) * (len(extent) - axis_at - 1))

    factor_of = one(*shards[0])
    for cut in shards[1:]:
        factor_of = factor_of * one(*cut)
    return factor_of


def bell_draw(rng, dims, deviation, reach, cuts=(), held_as=jnp.bfloat16):
    drawn = jax.random.normal(rng, dims, jnp.float32) * deviation
    if len(cuts) > 0:
        drawn = levels(rng, dims, cuts, -0.22, 0.18) * drawn
    return jnp.clip(drawn, min=-reach, max=reach).astype(held_as)


def setup_inputs(seed: int = 0) -> dict:
    key_list = jax.random.split(jax.random.key(seed), 11)
    return {
        "features": bell_draw(key_list[0], (NCX, NCY, NCZ, C, A), 1.0, 6.0, ((0, 8), (1, 4), (2, 8)), jnp.float32),
        "positions": jnp.clip(1.0 * jax.random.uniform(key_list[1], (NCX, NCY, NCZ, 3, A), jnp.float32) ** levels(key_list[1], (NCX, NCY, NCZ, 3, A), ((0, 8), (1, 4), (2, 8)), -0.2, 0.2), 0.0, 1.0),
        "counts": draw_counts(jax.random.fold_in(key_list[10], 71), 0),
        "waves": touch_ends(jax.random.randint(key_list[3], (3, K), -8, 9), jax.random.fold_in(key_list[3], 1), -8, 8).astype(jnp.int32),
        "filter_table": bell_draw(key_list[4], (K, C), 1.0, 6.0, (), jnp.float32),
        "w_value": bell_draw(key_list[5], (C, C), C ** -0.5, 0.5, (), jnp.float32),
        "w_charge": bell_draw(key_list[6], (C, C), C ** -0.5, 0.5, (), jnp.float32),
        "radial_mix": bell_draw(key_list[7], (B, C), B ** -0.5, 2.0, (), jnp.float32),
        "w_hidden": bell_draw(key_list[8], (C, F), C ** -0.5, 0.5, (), jnp.float32),
        "w_out": bell_draw(key_list[9], (F, C), F ** -0.5, 0.375, (), jnp.float32),
    }


highest = lax.Precision.HIGHEST
cut_radius = 1.0
message_scale = 0.125

def radial_kernel(own_pos, nearby_pos, shift, self_pair):
    offsets = shift[:, None, None] + nearby_pos[..., :, None, :] - own_pos[..., :, :, None]
    squared = lax.optimization_barrier(jnp.sum(offsets * offsets, axis=-3))
    distance = jnp.sqrt(squared)
    envelope = jnp.square(jnp.maximum(1.0 - squared / (cut_radius * cut_radius), 0.0))
    envelope = envelope * (1.0 - self_pair * jnp.eye(A, dtype=jnp.float32))
    centres = jnp.arange(B, dtype=jnp.float32) * (cut_radius / (B - 1))
    scaled = (distance[..., None, :, :] - centres[:, None, None]) * ((B - 1) / cut_radius)
    return jnp.exp(-scaled * scaled) * envelope[..., None, :, :]

def pair_term(own_pos, nearby, shift, self_pair, radial_mix):
    channels = nearby.shape[-2] - 3
    kernel = radial_kernel(own_pos, nearby[..., channels:, :], shift, self_pair)
    weighted = radial_mix[:, :, None] * nearby[..., None, :channels, :]
    return jnp.einsum('...bij,...bcj->...ci', kernel, weighted, precision=highest)

def short_range(values, positions, radial_mix):
    packed = jnp.concatenate([values, positions], axis=3)
    summed = jnp.zeros_like(values)
    for step in range(27):
        moves = (step // 9 - 1, step // 3 % 3 - 1, step % 3 - 1)
        nearby = jnp.roll(packed, (-moves[0], -moves[1], -moves[2]), axis=(0, 1, 2))
        shift = jnp.array(moves, dtype=jnp.float32)
        self_pair = 1.0 if step == 13 else 0.0
        pair_sum = lax.map(lambda slab_pair: pair_term(slab_pair[0], slab_pair[1], shift, self_pair, radial_mix), (positions, nearby))
        summed = summed + pair_sum
    return summed

def plane_waves(frac_x, frac_y, frac_z, waves):
    expand = (waves.shape[1],) + (1,) * frac_x.ndim
    wave_float = waves.astype(jnp.float32)
    angle = wave_float[0].reshape(expand) * frac_x + wave_float[1].reshape(expand) * frac_y + wave_float[2].reshape(expand) * frac_z
    angle = angle * (2.0 * math.pi)
    return (jnp.cos(angle), jnp.sin(angle))

def slab_waves(slab_index, slab_pos, waves):
    rows_y = jnp.arange(NCY, dtype=jnp.float32)[:, None, None]
    rows_z = jnp.arange(NCZ, dtype=jnp.float32)[None, :, None]
    frac_x = (slab_index.astype(jnp.float32) + slab_pos[:, :, 0, :]) / NCX
    frac_y = (rows_y + slab_pos[:, :, 1, :]) / NCY
    frac_z = (rows_z + slab_pos[:, :, 2, :]) / NCZ
    return plane_waves(frac_x, frac_y, frac_z, waves)

def long_range(charges, positions, waves, filter_table):
    slab_ids = jnp.arange(NCX, dtype=jnp.int32)

    def accumulate(summed, inputs):
        cosine, sine = slab_waves(inputs[0], inputs[1], waves)
        real_part = jnp.einsum('kyza,yzca->kc', cosine, inputs[2], precision=highest)
        imag_part = jnp.einsum('kyza,yzca->kc', sine, inputs[2], precision=highest)
        return (summed + jnp.stack([real_part, imag_part]), None)
    factors, unused = lax.scan(accumulate, jnp.zeros((2, K, C), jnp.float32), (slab_ids, positions, charges))
    normalizer = 1.0 / math.sqrt(NCX * NCY * NCZ * A)
    filtered = factors * normalizer * filter_table[None]

    def slab_potential(inputs):
        cosine, sine = slab_waves(inputs[0], inputs[1], waves)
        first = jnp.einsum('kc,kyza->yzca', filtered[0], cosine, precision=highest)
        second = jnp.einsum('kc,kyza->yzca', filtered[1], sine, precision=highest)
        return (first + second) * (1.0 / math.sqrt(K))
    return lax.map(slab_potential, (slab_ids, positions))

def reference(features, positions, counts, waves, filter_table, w_value, w_charge, radial_mix, w_hidden, w_out):
    slot_ids = lax.broadcasted_iota(jnp.int32, (NCX, NCY, NCZ, A), 3)
    present = (slot_ids < counts[..., None]).astype(jnp.float32)[..., None, :]
    values = jnp.einsum('dc,xyzda->xyzca', w_value, features, precision=highest) * present
    charges = jnp.einsum('dc,xyzda->xyzca', w_charge, features, precision=highest) * present
    messages = short_range(values, positions, radial_mix)
    potentials = long_range(charges, positions, waves, filter_table)
    mixed = features + message_scale * messages + potentials
    hidden = jax.nn.silu(jnp.einsum('cf,xyzca->xyzfa', w_hidden, mixed, precision=highest))
    return (mixed + jnp.einsum('fc,xyzfa->xyzca', w_out, hidden, precision=highest)) * present
```

```python
import math
import functools
import jax, jax.numpy as jnp, numpy as np
from jax import lax
from jax.experimental import pallas as pl
from jax.experimental.pallas import tpu as pltpu

f32 = jnp.float32
bf16 = jnp.bfloat16
NN = (((1,), (0,)), ((), ()))
NT = (((1,), (1,)), ((), ()))
TN = (((0,), (0,)), ((), ()))
LOG2E = 1.4426950408889634


def split(x):
    hi = x.astype(bf16)
    return hi, (x - hi.astype(f32)).astype(bf16)


def mm(a, b, dims):
    return lax.dot_general(a, b, dims, preferred_element_type=f32)


def mm3(a, b, dims):
    ah, al = split(a)
    bh, bl = split(b)
    return mm(ah, bh, dims) + (mm(ah, bl, dims) + mm(al, bh, dims))


def sincos(u):
    r = u - jnp.round(u)
    z = r * r
    s = jnp.full_like(z, S_C[-1])
    for c in S_C[-2::-1]:
        s = s * z + c
    s = s * r
    c_ = jnp.full_like(z, C_C[-1])
    for c in C_C[-2::-1]:
        c_ = c_ * z + c
    return 1.0 - 2.0 * (s * s), 2.0 * (s * c_)


def fit(fun, deg, lim):
    k = np.arange(200)
    z = 0.5 * lim * (1 - np.cos(np.pi * (k + 0.5) / 200))
    ch = np.polynomial.chebyshev.Chebyshev.fit(z, fun(z), deg, domain=[0, lim])
    return [float(v) for v in ch.convert(kind=np.polynomial.Polynomial).coef]


S_C = fit(lambda z: np.sinc(np.sqrt(z)) * np.pi, 4, 0.25)
C_C = fit(lambda z: np.cos(np.pi * np.sqrt(z)), 5, 0.25)


def phase_operand(pos_ref, cell0):
    rows = []
    for d, n in enumerate((16.0, 8.0, 8.0)):
        parts = []
        for p in range(4):
            off = (p // 2, p % 2, 0)[d]
            parts.append((pos_ref[p, d:d + 1, :] + (cell0[d] + off).astype(f32)) * (1.0 / n))
        v = jnp.concatenate(parts, axis=1)
        a = v.astype(bf16)
        v = v - a.astype(f32)
        b = v.astype(bf16)
        v = v - b.astype(f32)
        rows += [a, b, v.astype(bf16)]
    rows.append(jnp.zeros((7, 512), bf16))
    return jnp.concatenate(rows, axis=0)


def wave_operand(waves_ref, w16_ref):
    w = waves_ref[...].astype(f32)
    w16_ref[...] = jnp.concatenate(
        [w[d:d + 1] for d in range(3) for _ in range(3)] + [jnp.zeros((7, 2048), f32)], axis=0).astype(bf16)


def cell_origin():
    return (lax.axis_index("gx") * 2, lax.axis_index("gy") * 2, lax.axis_index("gz"))


def kernel_a(origin, feat, pos, counts, waves, wv, wc, hout, fout, w16, q2):
    wave_operand(waves, w16)
    lane = lax.broadcasted_iota(jnp.int32, (128, 128), 1)
    sub = lax.broadcasted_iota(jnp.int32, (128, 128), 0)
    for p in range(4):
        f = feat[p]
        n = counts[p]
        v = mm3(f, wv[...], TN)
        hout[p, 0:128, :] = jnp.where(sub < n, v, 0.0)
        hout[p, 128:136, :] = jnp.concatenate([pos[p], jnp.zeros((5, 128), f32)], axis=0)
        q = jnp.where(lane < n, mm3(wc[...], f, TN), 0.0)
        hi, lo = split(q)
        q2[0:128, p * 128:(p + 1) * 128] = hi
        q2[128:256, p * 128:(p + 1) * 128] = lo
    fr = phase_operand(pos, origin())

    def body(kb, _):
        u = mm(w16[:, pl.ds(pl.multiple_of(kb * 256, 256), 256)], fr, TN)
        c, s = sincos(u)
        for t, k in ((c, kb), (s, kb + 8)):
            th, tl = split(t)
            big = mm(q2[...], th, NT)
            fout[k] = big[0:128] + (big[128:256] + mm(q2[0:128], tl, NT))
        return 0
    lax.fori_loop(0, 8, body, 0)


def call_a(origin, feat, pos, counts, waves, wv, wc):
    V = pl.BlockSpec(memory_space=pltpu.VMEM)
    S = pl.BlockSpec(memory_space=pltpu.SMEM)
    return pl.pallas_call(
        functools.partial(kernel_a, origin),
        out_shape=(jax.ShapeDtypeStruct((4, 136, 128), f32), jax.ShapeDtypeStruct((16, 128, 256), f32)),
        in_specs=[V, V, S, V, V, V], out_specs=(V, V),
        scratch_shapes=[pltpu.VMEM((16, 2048), bf16), pltpu.VMEM((256, 512), bf16)],
        name="ka",
    )(feat, pos, counts, waves, wv, wc)


def kernel_c(origin, feat, pos, counts, waves, msg, fil, wh, wo, out, w16):
    wave_operand(waves, w16)
    fr = phase_operand(pos, origin())

    def body(kb, pot):
        u = mm(w16[:, pl.ds(pl.multiple_of(kb * 256, 256), 256)], fr, TN)
        c, s = sincos(u)
        for t, k in ((c, kb), (s, kb + 8)):
            th, tl = split(t)
            gh, gl = split(fil[k])
            big = mm(jnp.concatenate([gh, gl], axis=0), th, NN)
            pot = pot + (big[0:128] + (big[128:256] + mm(gh, tl, NN)))
        return pot
    pot = lax.fori_loop(0, 8, body, jnp.zeros((128, 512), f32))
    lane = lax.broadcasted_iota(jnp.int32, (128, 128), 1)
    for p in range(4):
        mixed = feat[p] + 0.125 * msg[p].T + pot[:, p * 128:(p + 1) * 128]
        h = mm3(wh[...], mixed, TN)
        h = h / (1.0 + jnp.exp(-h))
        o = mixed + mm3(wo[...], h, TN)
        out[p] = jnp.where(lane < counts[p], o, 0.0)


def call_c(origin, feat, pos, counts, waves, msg, fil, wh, wo):
    V = pl.BlockSpec(memory_space=pltpu.VMEM)
    S = pl.BlockSpec(memory_space=pltpu.SMEM)
    return pl.pallas_call(
        functools.partial(kernel_c, origin),
        out_shape=jax.ShapeDtypeStruct((4, 128, 128), f32),
        in_specs=[V, V, S, V, V, V, V, V], out_specs=V,
        scratch_shapes=[pltpu.VMEM((16, 2048), bf16)],
        name="kc",
    )(feat, pos, counts, waves, msg, fil, wh, wo)


IC = 32
SHIFTS = [(a, b, c) for a in range(3) for b in range(3) for c in range(3)]


def own_positions(H, PI, p):
    for d in range(3):
        row = H[1 + p // 2, 1 + p % 2, 1, 128 + d:129 + d, :]
        PI[p, d] = jnp.broadcast_to(row, (128, 128)).T


def make_vb(H, vb, x, y, z):
    hi, lo = split(H[x, y, z, 0:128, :])
    vb[x, y, z, :, 0:128] = hi
    vb[x, y, z, :, 128:256] = lo


def build(H, PI, K, p, px, py, ic, xs):
    i0 = pl.multiple_of(ic * IC, IC)
    own = [PI[p, d, pl.ds(i0, IC), :] for d in range(3)]
    for n, (a, b, c) in enumerate(SHIFTS):
        sft = (a - 1.0, b - 1.0, c - 1.0)
        r2 = None
        for d in range(3):
            row = H[px + a, py + b, c, 128 + d:129 + d, :] + sft[d]
            u = row - own[d]
            r2 = u * u if r2 is None else r2 + u * u
        e = jnp.maximum(1.0 - r2, 0.0)
        e = e * e
        if (a, b, c) == (1, 1, 1):
            ii = lax.broadcasted_iota(jnp.int32, (IC, 128), 0) + i0
            jj = lax.broadcasted_iota(jnp.int32, (IC, 128), 1)
            e = jnp.where(ii == jj, 0.0, e)
        rc = jnp.maximum(r2, 1e-30)
        w = jnp.exp2((rc * lax.rsqrt(rc)) * (14.0 * LOG2E))
        h = jnp.exp2(r2 * (-49.0 * LOG2E)) * e
        for k in range(8):
            hi, lo = split(h)
            K[k * IC:(k + 1) * IC, n * 128:(n + 1) * 128] = hi
            K[(k + 8) * IC:(k + 9) * IC, n * 128:(n + 1) * 128] = lo
            if k < 7:
                h = h * w


def multiply(vb, K, mix_ref, msg, p, px, py, ic):
    acc = None
    for a in range(3):
        v = vb[px + a, pl.ds(py, 3), :, :, :].reshape(1152, 256)
        t = mm(K[:, a * 1152:(a + 1) * 1152], v, NN)
        acc = t if acc is None else acc + t
    out = None
    for k in range(8):
        hh = acc[k * IC:(k + 1) * IC, :]
        t = hh[:, 0:128] + (hh[:, 128:256] + acc[(k + 8) * IC:(k + 9) * IC, 0:128])
        t = t * mix_ref[k:k + 1, :]
        out = t if out is None else out + t
    msg[p, pl.ds(pl.multiple_of(ic * IC, IC), IC), :] = out


def kernel_pairs(H, mix, msg, vb, PI, K, m8):
    for k in range(8):
        m8[k:k + 1, :] = mix[k:k + 1, :] * math.exp(-float(k * k))
    for p in range(4):
        own_positions(H, PI, p)

    def conv(n, _):
        make_vb(H, vb, n // 12, (n // 3) % 4, n % 3)
        return 0
    lax.fori_loop(0, 48, conv, 0)

    def body(t, _):
        p = t // (128 // IC)
        ic = t % (128 // IC)
        build(H, PI, K, p, p // 2, p % 2, ic, None)
        multiply(vb, K, m8, msg, p, p // 2, p % 2, ic)
        return 0
    lax.fori_loop(0, 4 * (128 // IC), body, 0)


def call_pairs(H, mix, kern=kernel_pairs, kslots=1):
    V = pl.BlockSpec(memory_space=pltpu.VMEM)
    return pl.pallas_call(
        kern,
        out_shape=jax.ShapeDtypeStruct((4, 128, 128), f32),
        in_specs=[V, V], out_specs=V,
        scratch_shapes=[pltpu.VMEM((4, 4, 3, 128, 256), bf16), pltpu.VMEM((4, 3, 128, 128), f32)]
        + [pltpu.VMEM((16 * IC, 3456), bf16)] * kslots + [pltpu.VMEM((8, 128), f32)],
        name="kpairs",
    )(H, mix)


MESH_ID = pl.DeviceIdType.MESH
FILTER_SCALE = 1.0 / math.sqrt(131072.0) / math.sqrt(2048.0)


class Place:
    def __init__(self):
        self.gx = lax.axis_index("gx")
        self.gy = lax.axis_index("gy")
        self.gz = lax.axis_index("gz")
        self.core = self.gx % 2
        self.zh = self.gx // 2
        self.x = self.gy
        self.y = self.gz // 2
        self.zl = self.gz % 2
        self.z = self.zh * 2 + self.zl

    def at_gx(self, v):
        return (v, self.gy, self.gz)

    def at_gy(self, v):
        return (self.gx, v, self.gz)

    def at_gz(self, v):
        return (self.gx, self.gy, v)

    def at_y(self, v):
        return (self.gx, self.gy, v * 2 + self.zl)

    def at_z(self, v):
        return (v // 2 * 2 + self.core, self.gy, self.y * 2 + v % 2)


def flip(v, bits):
    if bits == 1:
        return v + 1 - 2 * (v % 2)
    if bits == 3:
        return 3 - v
    return (v + 2) % 4


class Copies:
    def __init__(self, send, recv):
        self.send, self.recv, self.n, self.started = send, recv, 0, []

    def start(self, src, dst, device):
        i = self.n
        self.n += 1
        cp = pltpu.make_async_remote_copy(
            src_ref=src, dst_ref=dst, send_sem=self.send.at[i], recv_sem=self.recv.at[i],
            device_id=device, device_id_type=MESH_ID)
        cp.start()
        self.started.append(cp)
        return cp

    def finish(self):
        for cp in self.started:
            cp.wait_send()


def enter(me):
    bar = pltpu.get_barrier_semaphore()
    peers = [me.at_gx((me.gx + 1) % 8), me.at_gx((me.gx + 7) % 8),
             me.at_gy((me.gy + 1) % 4), me.at_gy((me.gy + 3) % 4),
             me.at_gz((me.gz + 2) % 8), me.at_gz((me.gz + 6) % 8)]
    peers += [me.at_z((me.z + i) % 8) for i in range(1, 8)]
    for p in peers:
        pl.semaphore_signal(bar, inc=1, device_id=p, device_id_type=MESH_ID)
    pl.semaphore_wait(bar, len(peers))


def halo_steps(me, cp, H):
    st = {}

    def h0():
        st["pair"] = cp.start(H.at[1:3, 1:3, 1], H.at[1:3, 1:3, 2 * me.zl], me.at_gz(me.gz + 1 - 2 * me.zl))

    def h1():
        st["pair"].wait_recv()
        st["fwd"] = cp.start(H.at[1:3, 1:3, 2 - 2 * me.zl], H.at[1:3, 1:3, 2 * me.zl],
                             me.at_gz((me.gz + 2 + 4 * me.zl) % 8))

    def h2():
        st["fwd"].wait_recv()
        up, down = me.at_gx((me.gx + 1) % 8), me.at_gx((me.gx + 7) % 8)
        st["gx"] = [cp.start(H.at[2, 1:3], H.at[0, 1:3], up), cp.start(H.at[1, 1:3], H.at[3, 1:3], down)]
        up, down = me.at_gy((me.gy + 1) % 4), me.at_gy((me.gy + 3) % 4)
        st["gy"] = [cp.start(H.at[1:3, 2], H.at[1:3, 0], up), cp.start(H.at[1:3, 1], H.at[1:3, 3], down)]

    def h3():
        for c in st["gx"]:
            c.wait_recv()
        up, down = me.at_gy((me.gy + 1) % 4), me.at_gy((me.gy + 3) % 4)
        for col in (0, 3):
            st["gy"].append(cp.start(H.at[col, 2], H.at[col, 0], up))
            st["gy"].append(cp.start(H.at[col, 1], H.at[col, 3], down))

    def h4():
        for c in st["gy"]:
            c.wait_recv()
    return [h0, h1, h2, h3, h4]


def reduce_steps(me, cp, F, G, R, filt):
    RD, R1, R2, R3, R4, RZ = R
    c64 = me.core * 64
    other = me.at_gx(me.gx + 1 - 2 * me.core)
    st = {}
    groups = []
    for g in range(4):
        bits = (1, 3) if g % 2 == 0 else (3, 1)
        rows = pl.ds(pl.multiple_of(c64 + 16 * g, 16), 16)
        axes = [(me.y, me.at_y), (me.x, me.at_gy)]
        if g >= 2:
            axes = axes[::-1]

        def view(ref, first, second, rows=rows, g=g):
            return ref.at[first, second, rows] if g < 2 else ref.at[second, first, rows]
        groups.append((g, bits, rows, axes, view))
    ALL = slice(None)

    def r0():
        for g in range(4):
            rows = pl.ds(pl.multiple_of(64 - c64 + 16 * g, 16), 16)
            st["D", g] = cp.start(F.at[:, :, rows], RD.at[g], other)

    def r1():
        for g, bits, rows, axes, view in groups:
            st["D", g].wait_recv()
            F[:, :, rows] = F[:, :, rows] + RD[g]
            v, at = axes[0]
            dev = at(flip(v, bits[0]))
            st["1", g] = [cp.start(view(F, flip(v, bits[0]), ALL), R1.at[g, 0], dev),
                          cp.start(view(F, flip(v, 2), ALL), R1.at[g, 1], dev)]

    def add(ref, first, second, val, g, rows):
        if g < 2:
            ref[first, second, rows] = ref[first, second, rows] + val
        else:
            ref[second, first, rows] = ref[second, first, rows] + val

    def r2():
        for g, bits, rows, axes, view in groups:
            v, at = axes[0]
            keep = (v, flip(v, bits[1]))
            for i in (1, 0):
                st["1", g][i].wait_recv()
                add(F, keep[i], ALL, R1[g, i], g, rows)
            st["2", g] = cp.start(view(F, keep[1], ALL), R2.at[g], at(flip(v, bits[1])))

    def r3():
        for g, bits, rows, axes, view in groups:
            v, at = axes[0]
            st["2", g].wait_recv()
            add(F, v, ALL, R2[g], g, rows)
            u, at = axes[1]
            dev = at(flip(u, bits[0]))
            st["3", g] = [cp.start(view(F, v, flip(u, bits[0])), R3.at[g, 0], dev),
                          cp.start(view(F, v, flip(u, 2)), R3.at[g, 1], dev)]

    def r4():
        for g, bits, rows, axes, view in groups:
            v = axes[0][0]
            u, at = axes[1]
            keep = (u, flip(u, bits[1]))
            for i in (1, 0):
                st["3", g][i].wait_recv()
                add(F, v, keep[i], R3[g, i], g, rows)
            st["4", g] = cp.start(view(F, v, keep[1]), R4.at[g], at(flip(u, bits[1])))

    def zrows(z):
        return pl.ds(pl.multiple_of(c64 + 8 * z, 8), 8)

    def r5():
        for g, bits, rows, axes, view in groups:
            st["4", g].wait_recv()
            add(F, axes[0][0], axes[1][0], R4[g], g, rows)
        for i in range(1, 8):
            z = (me.z + i) % 8
            st["z", i] = cp.start(F.at[me.y, me.x, zrows(z)], RZ.at[i], me.at_z(z))

    def r6():
        total = F[me.y, me.x, zrows(me.z)]
        for i in range(1, 8):
            st["z", i].wait_recv()
            total = total + RZ[i]
        G[me.y, me.x, zrows(me.z)] = total * filt()
        for i in range(1, 8):
            mine = G.at[me.y, me.x, zrows(me.z)]
            st["Z", i] = cp.start(mine, mine, me.at_z((me.z + i) % 8))

    def same(ref, dev):
        return cp.start(ref, ref, dev)

    def r7():
        for i in range(1, 8):
            st["Z", i].wait_recv()
        for g, bits, rows, axes, view in groups:
            v = axes[0][0]
            u, at = axes[1]
            st["4b", g] = same(view(G, v, u), at(flip(u, bits[1])))

    def r8():
        for g, bits, rows, axes, view in groups:
            v = axes[0][0]
            u, at = axes[1]
            st["4b", g].wait_recv()
            dev = at(flip(u, bits[0]))
            st["3b", g] = [same(view(G, v, u), dev), same(view(G, v, flip(u, bits[1])), dev)]

    def r9():
        for g, bits, rows, axes, view in groups:
            v, at = axes[0]
            for c in st["3b", g]:
                c.wait_recv()
            st["2b", g] = same(view(G, v, ALL), at(flip(v, bits[1])))

    def r10():
        for g, bits, rows, axes, view in groups:
            v, at = axes[0]
            st["2b", g].wait_recv()
            dev = at(flip(v, bits[0]))
            st["1b", g] = [same(view(G, v, ALL), dev), same(view(G, flip(v, bits[1]), ALL), dev)]

    def r11():
        for g, bits, rows, axes, view in groups:
            for c in st["1b", g]:
                c.wait_recv()
            st["Db", g] = same(G.at[:, :, rows], other)

    def r12():
        for g in range(4):
            st["Db", g].wait_recv()
    return [r0, r1, r2, r3, r4, r5, r6, r7, r8, r9, r10, r11, r12]


def kernel_b(hin, fin, filt_hbm, mix, msg, G, H, F, RD, R1, R2, R3, R4, RZ, fbuf, ftr, vb, PI, K, m8, send, recv, lsem):
    me = Place()
    kb = me.y * 4 + me.x
    local = [pltpu.make_async_copy(fin, F, lsem.at[0]),
             pltpu.make_async_copy(filt_hbm.at[pl.ds(pl.multiple_of((kb % 8) * 256, 256), 256)], fbuf, lsem.at[1])]
    local += [pltpu.make_async_copy(hin.at[p], H.at[1 + p // 2, 1 + p % 2, 1], lsem.at[2 + p]) for p in range(4)]
    for c in local:
        c.start()
    enter(me)
    for c in local:
        c.wait()
    cp = Copies(send, recv)

    def filt():
        ftr[...] = fbuf[...].T
        return ftr[pl.ds(pl.multiple_of(me.core * 64 + 8 * me.z, 8), 8), :] * FILTER_SCALE

    hs = halo_steps(me, cp, H)
    rs = reduce_steps(me, cp, F, G, (RD, R1, R2, R3, R4, RZ), filt)
    hs[0]()
    rs[0]()
    for k in range(8):
        m8[k:k + 1, :] = mix[k:k + 1, :] * math.exp(-float(k * k))
    for p in range(4):
        own_positions(H, PI, p)
    hs[1]()
    rs[1]()
    hs[2]()
    rs[2]()
    hs[3]()
    rs[3]()
    rs[4]()
    hs[4]()
    rs[5]()

    def conv(n, _):
        make_vb(H, vb, n // 12, (n // 3) % 4, n % 3)
        return 0
    lax.fori_loop(0, 48, conv, 0)
    rs[6]()

    def body(t, _):
        p = t // (128 // IC)
        ic = t % (128 // IC)
        build(H, PI, K, p, p // 2, p % 2, ic, None)
        multiply(vb, K, m8, msg, p, p // 2, p % 2, ic)
        return 0
    done = 0
    for step, until in zip(rs[7:], (2, 4, 6, 8, 11, 16)):
        lax.fori_loop(done, until, body, 0)
        done = until
        step()
    cp.finish()


NCOPY = 88


def call_b(hout, fout, filt, mix):
    V = pl.BlockSpec(memory_space=pltpu.VMEM)
    A = pl.BlockSpec(memory_space=pl.ANY)
    return pl.pallas_call(
        kernel_b,
        out_shape=(jax.ShapeDtypeStruct((4, 128, 128), f32), jax.ShapeDtypeStruct((4, 4, 128, 256), f32)),
        in_specs=[A, A, A, V], out_specs=(V, V),
        scratch_shapes=[
            pltpu.VMEM((4, 4, 3, 136, 128), f32), pltpu.VMEM((4, 4, 128, 256), f32),
            pltpu.VMEM((4, 4, 4, 16, 256), f32), pltpu.VMEM((4, 2, 4, 16, 256), f32),
            pltpu.VMEM((4, 4, 16, 256), f32), pltpu.VMEM((4, 2, 16, 256), f32),
            pltpu.VMEM((4, 16, 256), f32), pltpu.VMEM((8, 8, 256), f32),
            pltpu.VMEM((256, 128), f32), pltpu.VMEM((128, 256), f32),
            pltpu.VMEM((4, 4, 3, 128, 256), bf16), pltpu.VMEM((4, 3, 128, 128), f32),
            pltpu.VMEM((16 * IC, 3456), bf16), pltpu.VMEM((8, 128), f32),
            pltpu.SemaphoreType.DMA((NCOPY,)), pltpu.SemaphoreType.DMA((NCOPY,)), pltpu.SemaphoreType.DMA((6,)),
        ],
        compiler_params=pltpu.CompilerParams(collective_id=0, has_side_effects=True),
        name="kb",
    )(hout, fout.reshape(4, 4, 128, 256), filt, mix)


def shards(features, positions, counts, waves, filter_table, w_value, w_charge, radial_mix, w_hidden, w_out):
    feat = features.reshape(4, 128, 128)
    pos = positions.reshape(4, 3, 128)
    cnt = counts.reshape(4)
    hout, fout = call_a(cell_origin, feat, pos, cnt, waves, w_value, w_charge)
    msg, fil = call_b(hout, fout, filter_table, radial_mix)
    out = call_c(cell_origin, feat, pos, cnt, waves, msg, fil.reshape(16, 128, 256), w_hidden, w_out)
    return out.reshape(features.shape)


def solution(mesh):
    from jax.sharding import PartitionSpec as P
    cell = P("gx", "gy", "gz")
    five = P("gx", "gy", "gz", None, None)
    return jax.shard_map(
        shards, mesh=mesh,
        in_specs=(five, five, cell) + (P(),) * 7,
        out_specs=five, check_vma=False)
```

```python
import math
import functools
import jax, jax.numpy as jnp, numpy as np
from jax import lax
from jax.experimental import pallas as pl
from jax.experimental.pallas import tpu as pltpu
from jax.sharding import PartitionSpec as P

f32 = jnp.float32
bf16 = jnp.bfloat16
NN = (((1,), (0,)), ((), ()))
NT = (((1,), (1,)), ((), ()))
TN = (((0,), (0,)), ((), ()))
LOG2E = 1.4426950408889634
ALL = slice(None)


def split(x):
    hi = x.astype(bf16)
    return hi, (x - hi.astype(f32)).astype(bf16)


def mm(a, b, dims):
    return lax.dot_general(a, b, dims, preferred_element_type=f32)


def mm3(a, b, dims):
    ah, al = split(a)
    bh, bl = split(b)
    return mm(ah, bh, dims) + (mm(ah, bl, dims) + mm(al, bh, dims))


def fit(fun, deg, lim):
    k = np.arange(200)
    z = 0.5 * lim * (1 - np.cos(np.pi * (k + 0.5) / 200))
    ch = np.polynomial.chebyshev.Chebyshev.fit(z, fun(z), deg, domain=[0, lim])
    return [float(v) for v in ch.convert(kind=np.polynomial.Polynomial).coef]


S_C = fit(lambda z: math.sqrt(2.0) * np.sinc(np.sqrt(z)) * np.pi, 4, 0.25)
C_C = fit(lambda z: math.sqrt(2.0) * np.cos(np.pi * np.sqrt(z)), 4, 0.25)


def sincos(u):
    r = u - jnp.round(u)
    z = r * r
    s = S_C[3] + S_C[4] * z
    c = C_C[3] + C_C[4] * z
    for i in (2, 1, 0):
        s = s * z + S_C[i]
        c = c * z + C_C[i]
    s = s * r
    return 1.0 - s * s, s * c


def phase_operand(pos, cell0):
    rows = []
    for d, n in enumerate((16.0, 8.0, 8.0)):
        parts = []
        for p in range(4):
            off = (p // 2, p % 2, 0)[d]
            parts.append((pos[p // 2, p % 2, d] + (cell0[d] + off).astype(f32)) * (1.0 / n))
        v = jnp.concatenate(parts, axis=1)
        a = v.astype(bf16)
        v = v - a.astype(f32)
        b = v.astype(bf16)
        v = v - b.astype(f32)
        rows += [a, b, v.astype(bf16)]
    rows.append(jnp.zeros((7, 512), bf16))
    return jnp.concatenate(rows, axis=0)


def wave_operand(waves, w16):
    w = waves[...].astype(f32)
    w16[...] = jnp.concatenate(
        [w[d:d + 1] for d in range(3) for _ in range(3)] + [jnp.zeros((7, 2048), f32)], axis=0).astype(bf16)


IC = 32


def own_positions(H, PI, p):
    for d in range(3):
        row = H[1 + p // 2, 1 + p % 2, 1, 128 + d:129 + d, :]
        PI[p, d] = jnp.broadcast_to(row, (128, 128)).T


def make_vb(H, vb, x, y, z):
    hi, lo = split(H[x, y, z, 0:128, :])
    vb[x, y, z, :, 0:128] = hi
    vb[x, y, z, :, 128:256] = lo


def build(H, own, K, n, cell, shift, i0, is_self):
    x, y, z = cell
    r2 = None
    for d in range(3):
        row = H[x, y, z, 128 + d:129 + d, :] + shift[d]
        u = row - own[d]
        r2 = u * u if r2 is None else r2 + u * u
    e = jnp.maximum(1.0 - r2, 0.0)
    e = e * e
    if is_self is not None:
        ii = lax.broadcasted_iota(jnp.int32, (IC, 128), 0) + (i0 + jnp.where(is_self, 0, 1024))
        jj = lax.broadcasted_iota(jnp.int32, (IC, 128), 1)
        e = jnp.where(ii == jj, 0.0, e)
    rc = jnp.maximum(r2, 1e-30)
    w = jnp.exp2((rc * lax.rsqrt(rc)) * (14.0 * LOG2E))
    h = jnp.exp2(r2 * (-49.0 * LOG2E)) * e
    cols = slice(n * 128, (n + 1) * 128)
    for k in range(8):
        hi, lo = split(h)
        K[k * IC:(k + 1) * IC, cols] = hi
        K[(k + 8) * IC:(k + 9) * IC, cols] = lo
        if k < 7:
            h = h * w


def pair_unit(H, PI, vb, K, mix, msg, t, phase):
    p = t // (128 // IC)
    ic = t % (128 // IC)
    px, py = p // 2, p % 2
    i0 = pl.multiple_of(ic * IC, IC)
    own = [PI[p, d, pl.ds(i0, IC), :] for d in range(3)]
    if phase == 0:
        runs = [[(x, y, z) for y in (1, 2) for z in range(3)] for x in (1, 2)]
    elif phase == 1:
        runs = [[(x, 3 * py, z) for z in range(3)] for x in (1, 2)]
    else:
        runs = [[(3 * px, py + b, z) for b in range(3) for z in range(3)]]
    n = 0
    acc = None
    for run in runs:
        first = n
        for cell in run:
            x, y, z = cell
            shift = [jnp.asarray(x - 1 - px).astype(f32), jnp.asarray(y - 1 - py).astype(f32), z - 1.0]
            is_self = (p == (x - 1) * 2 + (y - 1)) if phase == 0 and z == 1 else None
            build(H, own, K, n, cell, shift, i0, is_self)
            n += 1
        x, y, _ = run[0]
        v = vb[x, pl.ds(y, len(run) // 3)].reshape(128 * len(run), 256)
        t_ = mm(K[:, first * 128:n * 128], v, NN)
        acc = t_ if acc is None else acc + t_
    out = None
    for k in range(8):
        hh = acc[k * IC:(k + 1) * IC, :]
        s = (hh[:, 0:128] + (hh[:, 128:256] + acc[(k + 8) * IC:(k + 9) * IC, 0:128])) * mix[k:k + 1, :]
        out = s if out is None else out + s
    rows = pl.ds(i0, IC)
    if phase == 0:
        msg[p, rows, :] = out
    else:
        msg[p, rows, :] = msg[p, rows, :] + out


MESH_ID = pl.DeviceIdType.MESH
FILTER_SCALE = 1.0 / math.sqrt(131072.0) / math.sqrt(2048.0)


class Place:
    def __init__(self):
        self.gx = lax.axis_index("gx")
        self.gy = lax.axis_index("gy")
        self.gz = lax.axis_index("gz")
        self.core = self.gx % 2
        self.zh = self.gx // 2
        self.x = self.gy
        self.y = self.gz // 2
        self.zl = self.gz % 2
        self.z = self.zh * 2 + self.zl

    def at_gx(self, v):
        return (v, self.gy, self.gz)

    def at_gy(self, v):
        return (self.gx, v, self.gz)

    def at_gz(self, v):
        return (self.gx, self.gy, v)

    def at_y(self, v):
        return (self.gx, self.gy, v * 2 + self.zl)

    def at_z(self, v):
        return (v // 2 * 2 + self.core, self.gy, self.y * 2 + v % 2)


def flip(v, bits):
    if bits == 1:
        return v + 1 - 2 * (v % 2)
    if bits == 3:
        return 3 - v
    return (v + 2) % 4


class Copies:
    def __init__(self, send, recv):
        self.send, self.recv, self.n, self.started = send, recv, 0, []

    def start(self, src, dst, device):
        i = self.n
        self.n += 1
        cp = pltpu.make_async_remote_copy(
            src_ref=src, dst_ref=dst, send_sem=self.send.at[i], recv_sem=self.recv.at[i],
            device_id=device, device_id_type=MESH_ID)
        cp.start()
        self.started.append(cp)
        return cp

    def finish(self):
        for cp in self.started:
            cp.wait_send()


def greet(me):
    bar = pltpu.get_barrier_semaphore()
    peers = [me.at_gx((me.gx + 1) % 8), me.at_gx((me.gx + 7) % 8),
             me.at_gy((me.gy + 1) % 4), me.at_gy((me.gy + 3) % 4),
             me.at_gz((me.gz + 2) % 8), me.at_gz((me.gz + 6) % 8)]
    peers += [me.at_z((me.z + i) % 8) for i in range(1, 8)]
    for p in peers:
        pl.semaphore_signal(bar, inc=1, device_id=p, device_id_type=MESH_ID)
    return lambda: pl.semaphore_wait(bar, len(peers))


def halo_steps(me, cp, H):
    st = {}
    up_y, down_y = me.at_gy((me.gy + 1) % 4), me.at_gy((me.gy + 3) % 4)
    up_x, down_x = me.at_gx((me.gx + 1) % 8), me.at_gx((me.gx + 7) % 8)

    def h0():
        st["pair"] = [cp.start(H.at[1 + p // 2, 1 + p % 2, 1], H.at[1 + p // 2, 1 + p % 2, 2 * me.zl],
                               me.at_gz(me.gz + 1 - 2 * me.zl)) for p in range(4)]
        st["gy"] = [cp.start(H.at[1:3, 2, 1], H.at[1:3, 0, 1], up_y),
                    cp.start(H.at[1:3, 1, 1], H.at[1:3, 3, 1], down_y)]

    def h1():
        st["fwd"] = []
        for p in range(4):
            st["pair"][p].wait_recv()
            c = (1 + p // 2, 1 + p % 2)
            st["fwd"].append(cp.start(H.at[c[0], c[1], 2 - 2 * me.zl], H.at[c[0], c[1], 2 * me.zl],
                                      me.at_gz((me.gz + 2 + 4 * me.zl) % 8)))

    def h2():
        for c in st["fwd"]:
            c.wait_recv()
        for z in (0, 2):
            st["gy"].append(cp.start(H.at[1:3, 2, z], H.at[1:3, 0, z], up_y))
            st["gy"].append(cp.start(H.at[1:3, 1, z], H.at[1:3, 3, z], down_y))
        st["gx"] = [cp.start(H.at[2, 1:3], H.at[0, 1:3], up_x), cp.start(H.at[1, 1:3], H.at[3, 1:3], down_x)]

    def h3():
        for c in st["gy"]:
            c.wait_recv()
        for y in (0, 3):
            st["gx"].append(cp.start(H.at[2, y], H.at[0, y], up_x))
            st["gx"].append(cp.start(H.at[1, y], H.at[3, y], down_x))

    def h4():
        for c in st["gx"]:
            c.wait_recv()
    return [h0, h1, h2, h3, h4]


def core_copy(me, F, RD, dsem, i):
    rows = pl.ds(pl.multiple_of(64 - me.core * 64, 64), 64)
    return pltpu.make_async_remote_copy(
        src_ref=F.at[i // 4, i % 4, :, rows], dst_ref=RD.at[i // 4, i % 4],
        send_sem=dsem.at[0, i], recv_sem=dsem.at[1, i],
        device_id=me.at_gx(me.gx + 1 - 2 * me.core), device_id_type=MESH_ID)


def reduce_steps(me, cp, Fs, Gs, Rs, dsem, filt, h):
    F, G = Fs.at[h], Gs.at[h]
    RD, R1, R2, R3, R4, RZ = [r.at[h] for r in Rs]
    c64 = me.core * 64
    other = me.at_gx(me.gx + 1 - 2 * me.core)
    st = {}
    groups = []
    for g in range(4):
        bits = (1, 3) if g % 2 == 0 else (3, 1)
        rows = pl.ds(pl.multiple_of(c64 + 16 * g, 16), 16)
        axes = [(me.y, me.at_y), (me.x, me.at_gy)]
        if g >= 2:
            axes = axes[::-1]

        def view(ref, first, second, rows=rows, g=g):
            return ref.at[first, second, rows] if g < 2 else ref.at[second, first, rows]
        groups.append((g, bits, rows, axes, view))

    def r1():
        for i in range(4 * h, 4 * h + 4):
            core_copy(me, Fs, Rs[0], dsem, i).wait_recv()
        for g, bits, rows, axes, view in groups:
            F[:, :, rows] = F[:, :, rows] + RD[:, :, 16 * g:16 * g + 16]
            v, at = axes[0]
            dev = at(flip(v, bits[0]))
            st["1", g] = [cp.start(view(F, flip(v, bits[0]), ALL), R1.at[g, 0], dev),
                          cp.start(view(F, flip(v, 2), ALL), R1.at[g, 1], dev)]

    def add(ref, first, second, val, g, rows):
        if g < 2:
            ref[first, second, rows] = ref[first, second, rows] + val
        else:
            ref[second, first, rows] = ref[second, first, rows] + val

    def r2():
        for g, bits, rows, axes, view in groups:
            v, at = axes[0]
            keep = (v, flip(v, bits[1]))
            for i in (1, 0):
                st["1", g][i].wait_recv()
                add(F, keep[i], ALL, R1[g, i], g, rows)
            st["2", g] = cp.start(view(F, keep[1], ALL), R2.at[g], at(flip(v, bits[1])))

    def r3():
        for g, bits, rows, axes, view in groups:
            v, at = axes[0]
            st["2", g].wait_recv()
            add(F, v, ALL, R2[g], g, rows)
            u, at = axes[1]
            dev = at(flip(u, bits[0]))
            st["3", g] = [cp.start(view(F, v, flip(u, bits[0])), R3.at[g, 0], dev),
                          cp.start(view(F, v, flip(u, 2)), R3.at[g, 1], dev)]

    def r4():
        for g, bits, rows, axes, view in groups:
            v = axes[0][0]
            u, at = axes[1]
            keep = (u, flip(u, bits[1]))
            for i in (1, 0):
                st["3", g][i].wait_recv()
                add(F, v, keep[i], R3[g, i], g, rows)
            st["4", g] = cp.start(view(F, v, keep[1]), R4.at[g], at(flip(u, bits[1])))

    def zrows(z):
        return pl.ds(pl.multiple_of(c64 + 8 * z, 8), 8)

    def r5():
        for g, bits, rows, axes, view in groups:
            st["4", g].wait_recv()
            add(F, axes[0][0], axes[1][0], R4[g], g, rows)
        for i in (4, 3, 5, 2, 6, 1, 7):
            z = (me.z + i) % 8
            st["z", i] = cp.start(F.at[me.y, me.x, zrows(z)], RZ.at[i], me.at_z(z))

    def r6():
        total = F[me.y, me.x, zrows(me.z)]
        for i in (1, 7, 2, 6, 3, 5, 4):
            st["z", i].wait_recv()
            total = total + RZ[i]
        G[me.y, me.x, zrows(me.z)] = total * filt()
        for i in (4, 3, 5, 2, 6, 1, 7):
            mine = G.at[me.y, me.x, zrows(me.z)]
            st["Z", i] = cp.start(mine, mine, me.at_z((me.z + i) % 8))

    def same(ref, dev):
        return cp.start(ref, ref, dev)

    def r7():
        for i in range(1, 8):
            st["Z", i].wait_recv()
        for g, bits, rows, axes, view in groups:
            v = axes[0][0]
            u, at = axes[1]
            st["4b", g] = same(view(G, v, u), at(flip(u, bits[1])))

    def r8():
        for g, bits, rows, axes, view in groups:
            v = axes[0][0]
            u, at = axes[1]
            st["4b", g].wait_recv()
            dev = at(flip(u, bits[0]))
            st["3b", g] = [same(view(G, v, u), dev), same(view(G, v, flip(u, bits[1])), dev)]

    def r9():
        for g, bits, rows, axes, view in groups:
            v, at = axes[0]
            for c in st["3b", g]:
                c.wait_recv()
            st["2b", g] = same(view(G, v, ALL), at(flip(v, bits[1])))

    def r10():
        st["Db"] = []
        for g, bits, rows, axes, view in groups:
            v, at = axes[0]
            st["2b", g].wait_recv()
            dev = at(flip(v, bits[0]))
            st["1b", g] = [same(view(G, v, ALL), dev), same(view(G, flip(v, bits[1]), ALL), dev)]
        for g, bits, rows, axes, view in groups:
            v = axes[0][0]
            for s in (v, flip(v, bits[1])):
                st["Db"].append(same(view(G, s, ALL), other))

    def r11():
        for g, bits, rows, axes, view in groups:
            v = axes[0][0]
            for c in st["1b", g]:
                c.wait_recv()
            for s in (flip(v, bits[0]), flip(v, 2)):
                st["Db"].append(same(view(G, s, ALL), other))

    def r12():
        for c in st["Db"]:
            c.wait_recv()
    return [None, r1, r2, r3, r4, r5, r6, r7, r8, r9, r10, r11, r12]


PLAN = [
    ("factors", 4, 6), ("r", 0, 1), ("factors", 6, 8), ("r", 1, 1), ("h", 1), ("r", 0, 2), ("h", 2), ("cA",), ("r", 1, 2), ("A", 2),
    ("r", 0, 3), ("A", 2), ("r", 1, 3), ("A", 2), ("r", 0, 4), ("A", 2), ("r", 1, 4), ("A", 1), ("r", 0, 5), ("A", 2), ("r", 1, 5),
    ("A", 3), ("h", 3), ("r", 0, 6), ("A", 2), ("r", 1, 6), ("cB",), ("B", 4), ("r", 0, 7), ("B", 4), ("r", 1, 7), ("B", 4),
    ("r", 0, 8), ("B", 4), ("r", 1, 8), ("h", 4), ("cC",), ("r", 0, 9), ("C", 3), ("r", 1, 9), ("C", 3), ("r", 0, 10), ("C", 3),
    ("r", 1, 10), ("C", 3), ("r", 0, 11), ("C", 4), ("r", 1, 11), ("r", 0, 12), ("pot", 0), ("r", 1, 12), ("pot", 1),
]


def kernel(feat, pos, counts, waves, filt_hbm, wv, wc, mix, wh, wo, out,
           H, F, G, RD, R1, R2, R3, R4, RZ, TH, TL, q2, w16, fbuf, ftr, vb, PI, K, m8, msg, potr,
           send, recv, dsem, lsem):
    me = Place()
    fcopy = [pltpu.make_async_copy(
        filt_hbm.at[pl.ds(pl.multiple_of((4 * h + me.y) * 256 + (me.x % 2) * 128, 128), 128)], fbuf.at[h], lsem.at[h])
        for h in range(2)]
    for c in fcopy:
        c.start()
    greeted = greet(me)
    lane = lax.broadcasted_iota(jnp.int32, (128, 128), 1)
    sub = lax.broadcasted_iota(jnp.int32, (128, 128), 0)
    cells = [(p // 2, p % 2, 0) for p in range(4)]
    for p, c in enumerate(cells):
        q = jnp.where(lane < counts[c[0], 0, c[1]], mm3(wc[...], feat[c], TN), 0.0)
        hi, lo = split(q)
        q2[0:128, p * 128:(p + 1) * 128] = hi
        q2[128:256, p * 128:(p + 1) * 128] = lo
        v = mm3(feat[c], wv[...], TN)
        H[1 + c[0], 1 + c[1], 1, 0:128, :] = jnp.where(sub < counts[c[0], 0, c[1]], v, 0.0)
        H[1 + c[0], 1 + c[1], 1, 128:136, :] = jnp.concatenate(
            [pos[c[0], c[1], d] for d in range(3)] + [jnp.zeros((5, 128), f32)], axis=0)
    wave_operand(waves, w16)
    fr = phase_operand(pos, (me.gx * 2, me.gy * 2, me.gz))

    def factors(i, send_now):
        u = mm(w16[:, pl.ds(pl.multiple_of(i * 256, 256), 256)], fr, TN)
        c, s = sincos(u)
        for t, k, x in ((c, i, 0), (s, i + 8, 2)):
            th, tl = split(t)
            TH[k] = th
            TL[k] = tl
            big = mm(q2[...], th, NT)
            f = big[0:128] + (big[128:256] + mm(q2[0:128], tl, NT))
            F[i // 4, i % 4, x] = f[:, 0:128]
            F[i // 4, i % 4, x + 1] = f[:, 128:256]
        if send_now:
            core_copy(me, F, RD, dsem, i).start()

    def factor_loop(lo, hi, send_now):
        def body(i, _):
            factors(i, send_now)
            return 0
        lax.fori_loop(lo, hi, body, 0)
    factor_loop(0, 4, False)
    for c in fcopy:
        c.wait()
    for h in range(2):
        ftr[h] = fbuf[h].T
    for k in range(8):
        m8[k:k + 1, :] = mix[k:k + 1, :] * math.exp(-float(k * k))
    for p in range(4):
        own_positions(H, PI, p)
    greeted()
    for i in range(4):
        core_copy(me, F, RD, dsem, i).start()
    cp = Copies(send, recv)
    hs = halo_steps(me, cp, H)
    hs[0]()

    def filt(h):
        return lambda: ftr[h, pl.ds(pl.multiple_of(me.core * 64 + 8 * me.z, 8), 8), :] * FILTER_SCALE

    rs = [reduce_steps(me, cp, F, G, (RD, R1, R2, R3, R4, RZ), dsem, filt(h), h) for h in range(2)]

    def convert(cells_of, n):
        def body(i, _):
            make_vb(H, vb, *cells_of(i))
            return 0
        lax.fori_loop(0, n, body, 0)

    def potential(h):
        def body(j, acc):
            y, t = j // 2, j % 2
            g = jnp.concatenate([G[h, y, 2 * t], G[h, y, 2 * t + 1]], axis=1)
            gh, gl = split(g)
            k = 4 * h + y + 8 * t
            big = mm(jnp.concatenate([gh, gl], axis=0), TH[k], NN)
            return acc + (big[0:128] + (big[128:256] + mm(gh, TL[k], NN)))
        potr[...] = lax.fori_loop(0, 8, body, potr[...] if h else jnp.zeros((128, 512), f32))

    at = {"A": 0, "B": 0, "C": 0}
    for item in PLAN:
        if item[0] == "h":
            hs[item[1]]()
        elif item[0] == "r":
            rs[item[1]][item[2]]()
        elif item[0] == "factors":
            factor_loop(item[1], item[2], True)
        elif item[0] == "pot":
            potential(item[1])
        elif item[0] == "cA":
            convert(lambda i: (1 + i // 6, 1 + (i // 3) % 2, i % 3), 12)
        elif item[0] == "cB":
            convert(lambda i: (1 + i // 6, 3 * ((i // 3) % 2), i % 3), 12)
        elif item[0] == "cC":
            convert(lambda i: (3 * (i // 12), (i // 3) % 4, i % 3), 24)
        else:
            def body(t, _, phase="ABC".index(item[0])):
                pair_unit(H, PI, vb, K, m8, msg, t, phase)
                return 0
            lax.fori_loop(at[item[0]], at[item[0]] + item[1], body, 0)
            at[item[0]] += item[1]
    assert all(v in (0, 16) for v in at.values())

    for p, c in enumerate(cells):
        mixed = feat[c] + 0.125 * msg[p].T + potr[:, p * 128:(p + 1) * 128]
        h = mm3(wh[...], mixed, TN)
        h = h / (1.0 + jnp.exp(-h))
        o = mixed + mm3(wo[...], h, TN)
        out[c] = jnp.where(lane < counts[c[0], 0, c[1]], o, 0.0)
    cp.finish()
    for i in range(8):
        core_copy(me, F, RD, dsem, i).wait_send()


NCOPY = 176


def shards(features, positions, counts, waves, filter_table, w_value, w_charge, radial_mix, w_hidden, w_out):
    V = pl.BlockSpec(memory_space=pltpu.VMEM)
    S = pl.BlockSpec(memory_space=pltpu.SMEM)
    A = pl.BlockSpec(memory_space=pl.ANY)
    vm = pltpu.VMEM
    return pl.pallas_call(
        kernel,
        out_shape=jax.ShapeDtypeStruct(features.shape, f32),
        in_specs=[V, V, S, V, A, V, V, V, V, V], out_specs=V,
        scratch_shapes=[
            vm((4, 4, 3, 136, 128), f32), vm((2, 4, 4, 128, 128), f32), vm((2, 4, 4, 128, 128), f32),
            vm((2, 4, 4, 64, 128), f32), vm((2, 4, 2, 4, 16, 128), f32),
            vm((2, 4, 4, 16, 128), f32), vm((2, 4, 2, 16, 128), f32),
            vm((2, 4, 16, 128), f32), vm((2, 8, 8, 128), f32),
            vm((16, 256, 512), bf16), vm((16, 256, 512), bf16), vm((256, 512), bf16), vm((16, 2048), bf16),
            vm((2, 128, 128), f32), vm((2, 128, 128), f32),
            vm((4, 4, 3, 128, 256), bf16), vm((4, 3, 128, 128), f32),
            vm((16 * IC, 1536), bf16), vm((8, 128), f32), vm((4, 128, 128), f32), vm((128, 512), f32),
            pltpu.SemaphoreType.DMA((NCOPY,)), pltpu.SemaphoreType.DMA((NCOPY,)),
            pltpu.SemaphoreType.DMA((2, 8)), pltpu.SemaphoreType.DMA((2,)),
        ],
        compiler_params=pltpu.CompilerParams(collective_id=0, has_side_effects=True),
        name="layer",
    )(features, positions.reshape(2, 2, 3, 1, 128), counts.reshape(2, 1, 2), waves, filter_table,
      w_value, w_charge, radial_mix, w_hidden, w_out)


def solution(mesh):
    cell = P("gx", "gy", "gz")
    five = P("gx", "gy", "gz", None, None)
    return jax.shard_map(
        shards, mesh=mesh,
        in_specs=(five, five, cell) + (P(),) * 7,
        out_specs=five, check_vma=False)
```

```python
import math
import functools
import jax, jax.numpy as jnp, numpy as np
from jax import lax
from jax.experimental import pallas as pl
from jax.experimental.pallas import tpu as pltpu
from jax.sharding import PartitionSpec as P

f32 = jnp.float32
bf16 = jnp.bfloat16
NN = (((1,), (0,)), ((), ()))
NT = (((1,), (1,)), ((), ()))
TN = (((0,), (0,)), ((), ()))
LOG2E = 1.4426950408889634
ALL = slice(None)


def split(x):
    hi = x.astype(bf16)
    return hi, (x - hi.astype(f32)).astype(bf16)


def mm(a, b, dims):
    return lax.dot_general(a, b, dims, preferred_element_type=f32)


def mm3(a, b, dims):
    ah, al = split(a)
    bh, bl = split(b)
    return mm(ah, bh, dims) + (mm(ah, bl, dims) + mm(al, bh, dims))


def fit(fun, deg, lim):
    k = np.arange(200)
    z = 0.5 * lim * (1 - np.cos(np.pi * (k + 0.5) / 200))
    ch = np.polynomial.chebyshev.Chebyshev.fit(z, fun(z), deg, domain=[0, lim])
    return [float(v) for v in ch.convert(kind=np.polynomial.Polynomial).coef]


S_C = fit(lambda z: math.sqrt(2.0) * np.sinc(np.sqrt(z)) * np.pi, 4, 0.25)
C_C = fit(lambda z: math.sqrt(2.0) * np.cos(np.pi * np.sqrt(z)), 4, 0.25)


def sincos(u):
    r = u - jnp.round(u)
    z = r * r
    s = S_C[3] + S_C[4] * z
    c = C_C[3] + C_C[4] * z
    for i in (2, 1, 0):
        s = s * z + S_C[i]
        c = c * z + C_C[i]
    s = s * r
    return 1.0 - s * s, s * c


def phase_operand(pos, cell0):
    rows = []
    for d, n in enumerate((16.0, 8.0, 8.0)):
        parts = []
        for p in range(4):
            off = (p // 2, p % 2, 0)[d]
            parts.append((pos[p // 2, p % 2, d] + (cell0[d] + off).astype(f32)) * (1.0 / n))
        v = jnp.concatenate(parts, axis=1)
        a = v.astype(bf16)
        v = v - a.astype(f32)
        b = v.astype(bf16)
        v = v - b.astype(f32)
        rows += [a, b, v.astype(bf16)]
    rows.append(jnp.zeros((7, 512), bf16))
    return jnp.concatenate(rows, axis=0)


def wave_operand(waves, w16):
    w = waves[...].astype(f32)
    w16[...] = jnp.concatenate(
        [w[d:d + 1] for d in range(3) for _ in range(3)] + [jnp.zeros((7, 2048), f32)], axis=0).astype(bf16)


IC = 32


def own_positions(H, PI, p):
    for d in range(3):
        row = H[1 + p // 2, 1 + p % 2, 1, 128 + d:129 + d, :]
        PI[p, d] = jnp.broadcast_to(row, (128, 128)).T


OWN_CELLS = [(x, y, 1) for x in (1, 2) for y in (1, 2)] + [(x, y, z) for x in (1, 2) for y in (1, 2) for z in (0, 2)]


def make_vb(H, dst, at, x, y, z):
    hi, lo = split(H[x, y, z, 0:128, :])
    dst[at + (ALL, slice(0, 128))] = hi
    dst[at + (ALL, slice(128, 256))] = lo


def build(H, own, K, n, cell, shift, i0, is_self):
    x, y, z = cell
    r2 = None
    for d in range(3):
        row = H[x, y, z, 128 + d:129 + d, :] + shift[d]
        u = row - own[d]
        r2 = u * u if r2 is None else r2 + u * u
    e = jnp.maximum(1.0 - r2, 0.0)
    e = e * e
    if is_self is not None:
        ii = lax.broadcasted_iota(jnp.int32, (IC, 128), 0) + (i0 + jnp.where(is_self, 0, 1024))
        jj = lax.broadcasted_iota(jnp.int32, (IC, 128), 1)
        e = jnp.where(ii == jj, 0.0, e)
    rc = jnp.maximum(r2, 1e-30)
    w = jnp.exp2((rc * lax.rsqrt(rc)) * (14.0 * LOG2E))
    h = jnp.exp2(r2 * (-49.0 * LOG2E)) * e
    cols = slice(n * 128, (n + 1) * 128)
    for k in range(8):
        hi, lo = split(h)
        K[k * IC:(k + 1) * IC, cols] = hi
        K[(k + 8) * IC:(k + 9) * IC, cols] = lo
        if k < 7:
            h = h * w


def pair_unit(H, PI, va, vb, K, mix, msg, t, phase):
    p = t // (128 // IC)
    ic = t % (128 // IC)
    px, py = p // 2, p % 2
    i0 = pl.multiple_of(ic * IC, IC)
    own = [PI[p, d, pl.ds(i0, IC), :] for d in range(3)]
    if phase == 0:
        runs = [OWN_CELLS[0:4]]
    elif phase == 1:
        runs = [OWN_CELLS[4:12]]
    elif phase == 2:
        runs = [[(x, 3 * py, z) for z in range(3)] for x in (1, 2)]
    else:
        runs = [[(3 * px, py + b, z) for b in range(3) for z in range(3)]]
    n = 0
    acc = None
    for run in runs:
        first = n
        for cell in run:
            x, y, z = cell
            shift = [jnp.asarray(x - 1 - px).astype(f32), jnp.asarray(y - 1 - py).astype(f32), z - 1.0]
            is_self = (p == (x - 1) * 2 + (y - 1)) if phase == 0 else None
            build(H, own, K, n, cell, shift, i0, is_self)
            n += 1
        x, y, _ = run[0]
        if phase < 2:
            v = va[4 * phase:4 * phase + len(run)].reshape(128 * len(run), 256)
        else:
            v = vb[x, pl.ds(y, len(run) // 3)].reshape(128 * len(run), 256)
        t_ = mm(K[:, first * 128:n * 128], v, NN)
        acc = t_ if acc is None else acc + t_
    out = None
    for k in range(8):
        hh = acc[k * IC:(k + 1) * IC, :]
        s = (hh[:, 0:128] + (hh[:, 128:256] + acc[(k + 8) * IC:(k + 9) * IC, 0:128])) * mix[k:k + 1, :]
        out = s if out is None else out + s
    rows = pl.ds(i0, IC)
    if phase == 0:
        msg[p, rows, :] = out
    else:
        msg[p, rows, :] = msg[p, rows, :] + out


MESH_ID = pl.DeviceIdType.MESH
FILTER_SCALE = 1.0 / math.sqrt(131072.0) / math.sqrt(2048.0)


class Place:
    def __init__(self):
        self.gx = lax.axis_index("gx")
        self.gy = lax.axis_index("gy")
        self.gz = lax.axis_index("gz")
        self.core = self.gx % 2
        self.zh = self.gx // 2
        self.x = self.gy
        self.y = self.gz // 2
        self.zl = self.gz % 2
        self.z = self.zh * 2 + self.zl

    def at_gx(self, v):
        return (v, self.gy, self.gz)

    def at_gy(self, v):
        return (self.gx, v, self.gz)

    def at_gz(self, v):
        return (self.gx, self.gy, v)

    def at_y(self, v):
        return (self.gx, self.gy, v * 2 + self.zl)

    def at_z(self, v):
        return (v // 2 * 2 + self.core, self.gy, self.y * 2 + v % 2)


def flip(v, bits):
    if bits == 1:
        return v + 1 - 2 * (v % 2)
    if bits == 3:
        return 3 - v
    return (v + 2) % 4


class Copies:
    def __init__(self, send, recv):
        self.send, self.recv, self.n, self.started = send, recv, 0, []

    def start(self, src, dst, device):
        i = self.n
        self.n += 1
        cp = pltpu.make_async_remote_copy(
            src_ref=src, dst_ref=dst, send_sem=self.send.at[i], recv_sem=self.recv.at[i],
            device_id=device, device_id_type=MESH_ID)
        cp.start()
        self.started.append(cp)
        return cp

    def finish(self):
        for cp in self.started:
            cp.wait_send()


def greet(me):
    bar = pltpu.get_barrier_semaphore()
    peers = [me.at_gx((me.gx + 1) % 8), me.at_gx((me.gx + 7) % 8),
             me.at_gy((me.gy + 1) % 4), me.at_gy((me.gy + 3) % 4),
             me.at_gz((me.gz + 2) % 8), me.at_gz((me.gz + 6) % 8),
             me.at_gy((me.gy + 2) % 4), me.at_gz((me.gz + 4) % 8)]
    peers += [me.at_z((me.z + i) % 8) for i in range(1, 8)]
    for p in peers:
        pl.semaphore_signal(bar, inc=1, device_id=p, device_id_type=MESH_ID)
    return lambda: pl.semaphore_wait(bar, len(peers))


def halo_steps(me, cp, H):
    st = {}
    up_y, down_y = me.at_gy((me.gy + 1) % 4), me.at_gy((me.gy + 3) % 4)
    up_x, down_x = me.at_gx((me.gx + 1) % 8), me.at_gx((me.gx + 7) % 8)

    def h0():
        st["pair"] = [cp.start(H.at[1 + p // 2, 1 + p % 2, 1], H.at[1 + p // 2, 1 + p % 2, 2 * me.zl],
                               me.at_gz(me.gz + 1 - 2 * me.zl)) for p in range(4)]
        st["gy"] = [cp.start(H.at[1:3, 2, 1], H.at[1:3, 0, 1], up_y),
                    cp.start(H.at[1:3, 1, 1], H.at[1:3, 3, 1], down_y)]

    def h1():
        st["fwd"] = []
        for p in range(4):
            st["pair"][p].wait_recv()
            c = (1 + p // 2, 1 + p % 2)
            st["fwd"].append(cp.start(H.at[c[0], c[1], 2 - 2 * me.zl], H.at[c[0], c[1], 2 * me.zl],
                                      me.at_gz((me.gz + 2 + 4 * me.zl) % 8)))

    def h2():
        for c in st["fwd"]:
            c.wait_recv()
        st["gx"] = [cp.start(H.at[1 + me.core, 1:3], H.at[3 - 3 * me.core, 1:3], me.at_gx((me.gx + 7 + 2 * me.core) % 8)),
                    cp.start(H.at[2 - me.core, 1:3], H.at[3 * me.core, 1:3], me.at_gx(me.gx + 1 - 2 * me.core))]

    def h3():
        for z in (0, 2):
            st["gy"].append(cp.start(H.at[1:3, 2, z], H.at[1:3, 0, z], up_y))
            st["gy"].append(cp.start(H.at[1:3, 1, z], H.at[1:3, 3, z], down_y))

    def h4():
        for c in st["gx"]:
            c.wait_recv()
        far = 3 * me.core
        st["corner"] = [cp.start(H.at[far, 2], H.at[far, 0], up_y), cp.start(H.at[far, 1], H.at[far, 3], down_y)]

    def h5():
        for c in st["gy"]:
            c.wait_recv()
        for y in (0, 3):
            st["corner"].append(cp.start(H.at[2 - me.core, y], H.at[3 * me.core, y], me.at_gx(me.gx + 1 - 2 * me.core)))

    def h6():
        for c in st["corner"]:
            c.wait_recv()
    return [h0, h1, h2, h3, h4, h5, h6]


def core_copy(me, F, RD, dsem, i):
    rows = pl.ds(pl.multiple_of(64 - me.core * 64, 64), 64)
    return pltpu.make_async_remote_copy(
        src_ref=F.at[i // 4, i % 4, :, rows], dst_ref=RD.at[i // 4, i % 4],
        send_sem=dsem.at[0, i], recv_sem=dsem.at[1, i],
        device_id=me.at_gx(me.gx + 1 - 2 * me.core), device_id_type=MESH_ID)


def reduce_steps(me, cp, Fs, Gs, Rs, dsem, filt, h):
    F, G = Fs.at[h], Gs.at[h]
    RD, R1, R2, R3, RZ = [r.at[h] for r in Rs]
    c64 = me.core * 64
    other = me.at_gx(me.gx + 1 - 2 * me.core)
    st = {}
    groups = []
    for g in range(4):
        bits = (1, 3) if g % 2 == 0 else (3, 1)
        rows = pl.ds(pl.multiple_of(c64 + 16 * g, 16), 16)
        axes = [(me.y, me.at_y), (me.x, me.at_gy)]
        if g >= 2:
            axes = axes[::-1]

        def view(ref, first, second, rows=rows, g=g):
            return ref.at[first, second, rows] if g < 2 else ref.at[second, first, rows]
        groups.append((g, bits, rows, axes, view))

    def r1():
        for i in range(4 * h, 4 * h + 4):
            core_copy(me, Fs, Rs[0], dsem, i).wait_recv()
        for g, bits, rows, axes, view in groups:
            F[:, :, rows] = F[:, :, rows] + RD[:, :, 16 * g:16 * g + 16]
            v, at = axes[0]
            dev = at(flip(v, bits[0]))
            st["1", g] = [cp.start(view(F, flip(v, bits[0]), ALL), R1.at[g, 0], dev),
                          cp.start(view(F, flip(v, 2), ALL), R1.at[g, 1], dev)]

    def add(ref, first, second, val, g, rows):
        if g < 2:
            ref[first, second, rows] = ref[first, second, rows] + val
        else:
            ref[second, first, rows] = ref[second, first, rows] + val

    def r2():
        for g, bits, rows, axes, view in groups:
            v, at = axes[0]
            keep = (v, flip(v, bits[1]))
            for i in (1, 0):
                st["1", g][i].wait_recv()
                add(F, keep[i], ALL, R1[g, i], g, rows)
            st["2", g] = cp.start(view(F, keep[1], ALL), R2.at[g], at(flip(v, bits[1])))

    def r3():
        for g, bits, rows, axes, view in groups:
            v, at = axes[0]
            st["2", g].wait_recv()
            add(F, v, ALL, R2[g], g, rows)
            u, at = axes[1]
            st["3", g] = [cp.start(view(F, v, (u + i) % 4), R3.at[g, i - 1], at((u + i) % 4)) for i in (2, 1, 3)]

    def zrows(z):
        return pl.ds(pl.multiple_of(c64 + 8 * z, 8), 8)

    def r4():
        for g, bits, rows, axes, view in groups:
            for c in st["3", g]:
                c.wait_recv()
            add(F, axes[0][0], axes[1][0], R3[g, 0] + (R3[g, 1] + R3[g, 2]), g, rows)
        for i in (4, 3, 5, 2, 6, 1, 7):
            z = (me.z + i) % 8
            st["z", i] = cp.start(F.at[me.y, me.x, zrows(z)], RZ.at[i], me.at_z(z))

    def r5():
        total = F[me.y, me.x, zrows(me.z)]
        for i in (1, 7, 2, 6, 3, 5, 4):
            st["z", i].wait_recv()
            total = total + RZ[i]
        G[me.y, me.x, zrows(me.z)] = total * filt()
        for i in (4, 3, 5, 2, 6, 1, 7):
            mine = G.at[me.y, me.x, zrows(me.z)]
            st["Z", i] = cp.start(mine, mine, me.at_z((me.z + i) % 8))

    def same(ref, dev):
        return cp.start(ref, ref, dev)

    def r6():
        for i in range(1, 8):
            st["Z", i].wait_recv()
        for g, bits, rows, axes, view in groups:
            u, at = axes[1]
            st["3b", g] = [same(view(G, axes[0][0], u), at((u + i) % 4)) for i in (2, 1, 3)]

    def r7():
        for g, bits, rows, axes, view in groups:
            v, at = axes[0]
            for c in st["3b", g]:
                c.wait_recv()
            st["2b", g] = same(view(G, v, ALL), at(flip(v, bits[1])))

    def r8():
        st["Db"] = []
        for g, bits, rows, axes, view in groups:
            v, at = axes[0]
            st["2b", g].wait_recv()
            dev = at(flip(v, bits[0]))
            st["1b", g] = [same(view(G, v, ALL), dev), same(view(G, flip(v, bits[1]), ALL), dev)]
        for g, bits, rows, axes, view in groups:
            v = axes[0][0]
            for s in (v, flip(v, bits[1])):
                st["Db"].append(same(view(G, s, ALL), other))

    def r9():
        for g, bits, rows, axes, view in groups:
            v = axes[0][0]
            for c in st["1b", g]:
                c.wait_recv()
            for s in (flip(v, bits[0]), flip(v, 2)):
                st["Db"].append(same(view(G, s, ALL), other))

    def r10():
        for c in st["Db"]:
            c.wait_recv()
    return [None, r1, r2, r3, r4, r5, r6, r7, r8, r9, r10]


EVENTS = [
    "f46", "r01", "f68", "r11", "ca", "a4", "h1", "r02", "a4", "r12", "a4", "h2", "cA", "r03", "A1", "r13",
    "a4", "r04", "h3", "A3", "r14", "A4", "r05", "h4", "A3", "r15", "A3", "r06", "h5", "cB", "A2", "r16",
    "B4", "r07", "B4", "r17", "B4", "r08", "B4", "r18", "h6", "cC", "C3", "r09", "C3", "r19", "C3", "r010",
    "p0", "C3", "r110", "C4", "p1",
]


def parse(events):
    for w in events:
        if w[0] == "r":
            yield "r", int(w[1]), int(w[2:])
        elif w[0] == "f":
            yield "factors", int(w[1]), int(w[2])
        elif w[0] == "p":
            yield "pot", int(w[1])
        elif w[0] == "c":
            yield (w,)
        else:
            yield {"h": "h", "a": 0, "A": 1, "B": 2, "C": 3}[w[0]], int(w[1:])


PLAN = list(parse(EVENTS))


def kernel(feat, pos, counts, waves, filt_hbm, wv, wc, mix, wh, wo, out,
           H, F, G, RD, R1, R2, R3, RZ, TH, TL, q2, w16, fbuf, ftr, va, vb, PI, K, m8, msg, potr,
           send, recv, dsem, lsem):
    me = Place()
    fcopy = [pltpu.make_async_copy(
        filt_hbm.at[pl.ds(pl.multiple_of((4 * h + me.y) * 256 + (me.x % 2) * 128, 128), 128)], fbuf.at[h], lsem.at[h])
        for h in range(2)]
    for c in fcopy:
        c.start()
    greeted = greet(me)
    lane = lax.broadcasted_iota(jnp.int32, (128, 128), 1)
    sub = lax.broadcasted_iota(jnp.int32, (128, 128), 0)
    cells = [(p // 2, p % 2, 0) for p in range(4)]
    for p, c in enumerate(cells):
        q = jnp.where(lane < counts[c[0], 0, c[1]], mm3(wc[...], feat[c], TN), 0.0)
        hi, lo = split(q)
        q2[0:128, p * 128:(p + 1) * 128] = hi
        q2[128:256, p * 128:(p + 1) * 128] = lo
        v = mm3(feat[c], wv[...], TN)
        H[1 + c[0], 1 + c[1], 1, 0:128, :] = jnp.where(sub < counts[c[0], 0, c[1]], v, 0.0)
        H[1 + c[0], 1 + c[1], 1, 128:136, :] = jnp.concatenate(
            [pos[c[0], c[1], d] for d in range(3)] + [jnp.zeros((5, 128), f32)], axis=0)
    wave_operand(waves, w16)
    fr = phase_operand(pos, (me.gx * 2, me.gy * 2, me.gz))

    def factors(i, send_now):
        u = mm(w16[:, pl.ds(pl.multiple_of(i * 256, 256), 256)], fr, TN)
        c, s = sincos(u)
        for t, k, x in ((c, i, 0), (s, i + 8, 2)):
            th, tl = split(t)
            TH[k] = th
            TL[k] = tl
            big = mm(q2[...], th, NT)
            f = big[0:128] + (big[128:256] + mm(q2[0:128], tl, NT))
            F[i // 4, i % 4, x] = f[:, 0:128]
            F[i // 4, i % 4, x + 1] = f[:, 128:256]
        if send_now:
            core_copy(me, F, RD, dsem, i).start()

    def factor_loop(lo, hi, send_now):
        def body(i, _):
            factors(i, send_now)
            return 0
        lax.fori_loop(lo, hi, body, 0)
    factor_loop(0, 4, False)
    for c in fcopy:
        c.wait()
    for h in range(2):
        ftr[h] = fbuf[h].T
    for k in range(8):
        m8[k:k + 1, :] = mix[k:k + 1, :] * math.exp(-float(k * k))
    for p in range(4):
        own_positions(H, PI, p)
    greeted()
    for i in range(4):
        core_copy(me, F, RD, dsem, i).start()
    cp = Copies(send, recv)
    hs = halo_steps(me, cp, H)
    hs[0]()

    def filt(h):
        return lambda: ftr[h, pl.ds(pl.multiple_of(me.core * 64 + 8 * me.z, 8), 8), :] * FILTER_SCALE

    rs = [reduce_steps(me, cp, F, G, (RD, R1, R2, R3, RZ), dsem, filt(h), h) for h in range(2)]

    def convert(cells_of, n):
        def body(i, _):
            c = cells_of(i)
            make_vb(H, vb, c, *c)
            return 0
        lax.fori_loop(0, n, body, 0)

    def potential(h):
        def body(j, acc):
            y, t = j // 2, j % 2
            g = jnp.concatenate([G[h, y, 2 * t], G[h, y, 2 * t + 1]], axis=1)
            gh, gl = split(g)
            k = 4 * h + y + 8 * t
            big = mm(jnp.concatenate([gh, gl], axis=0), TH[k], NN)
            return acc + (big[0:128] + (big[128:256] + mm(gh, TL[k], NN)))
        potr[...] = lax.fori_loop(0, 8, body, potr[...] if h else jnp.zeros((128, 512), f32))

    at = [0, 0, 0, 0]
    for item in PLAN:
        if item[0] == "h":
            hs[item[1]]()
        elif item[0] == "r":
            rs[item[1]][item[2]]()
        elif item[0] == "factors":
            factor_loop(item[1], item[2], True)
        elif item[0] == "pot":
            potential(item[1])
        elif item[0] == "ca":
            for n in range(4):
                make_vb(H, va, (n,), *OWN_CELLS[n])
        elif item[0] == "cA":
            for n in range(4, 12):
                make_vb(H, va, (n,), *OWN_CELLS[n])
        elif item[0] == "cB":
            convert(lambda i: (1 + i // 6, 3 * ((i // 3) % 2), i % 3), 12)
        elif item[0] == "cC":
            convert(lambda i: (3 * (i // 12), (i // 3) % 4, i % 3), 24)
        else:
            def body(t, _, phase=item[0]):
                pair_unit(H, PI, va, vb, K, m8, msg, t, phase)
                return 0
            lax.fori_loop(at[item[0]], at[item[0]] + item[1], body, 0)
            at[item[0]] += item[1]

    for p, c in enumerate(cells):
        mixed = feat[c] + 0.125 * msg[p].T + potr[:, p * 128:(p + 1) * 128]
        h = mm3(wh[...], mixed, TN)
        h = h / (1.0 + jnp.exp(-h))
        o = mixed + mm3(wo[...], h, TN)
        out[c] = jnp.where(lane < counts[c[0], 0, c[1]], o, 0.0)
    cp.finish()
    for i in range(8):
        core_copy(me, F, RD, dsem, i).wait_send()


NCOPY = 176


def shards(features, positions, counts, waves, filter_table, w_value, w_charge, radial_mix, w_hidden, w_out):
    V = pl.BlockSpec(memory_space=pltpu.VMEM)
    S = pl.BlockSpec(memory_space=pltpu.SMEM)
    A = pl.BlockSpec(memory_space=pl.ANY)
    vm = pltpu.VMEM
    return pl.pallas_call(
        kernel,
        out_shape=jax.ShapeDtypeStruct(features.shape, f32),
        in_specs=[V, V, S, V, A, V, V, V, V, V], out_specs=V,
        scratch_shapes=[
            vm((4, 4, 3, 136, 128), f32), vm((2, 4, 4, 128, 128), f32), vm((2, 4, 4, 128, 128), f32),
            vm((2, 4, 4, 64, 128), f32), vm((2, 4, 2, 4, 16, 128), f32),
            vm((2, 4, 4, 16, 128), f32), vm((2, 4, 3, 16, 128), f32),
            vm((2, 8, 8, 128), f32),
            vm((16, 256, 512), bf16), vm((16, 256, 512), bf16), vm((256, 512), bf16), vm((16, 2048), bf16),
            vm((2, 128, 128), f32), vm((2, 128, 128), f32),
            vm((12, 128, 256), bf16), vm((4, 4, 3, 128, 256), bf16), vm((4, 3, 128, 128), f32),
            vm((16 * IC, 1152), bf16), vm((8, 128), f32), vm((4, 128, 128), f32), vm((128, 512), f32),
            pltpu.SemaphoreType.DMA((NCOPY,)), pltpu.SemaphoreType.DMA((NCOPY,)),
            pltpu.SemaphoreType.DMA((2, 8)), pltpu.SemaphoreType.DMA((2,)),
        ],
        compiler_params=pltpu.CompilerParams(collective_id=0, has_side_effects=True),
        name="layer",
    )(features, positions.reshape(2, 2, 3, 1, 128), counts.reshape(2, 1, 2), waves, filter_table,
      w_value, w_charge, radial_mix, w_hidden, w_out)


def solution(mesh):
    cell = P("gx", "gy", "gz")
    five = P("gx", "gy", "gz", None, None)
    return jax.shard_map(
        shards, mesh=mesh,
        in_specs=(five, five, cell) + (P(),) * 7,
        out_specs=five, check_vma=False)
```

```python
import math
import functools
import jax, jax.numpy as jnp, numpy as np
from jax import lax
from jax.experimental import pallas as pl
from jax.experimental.pallas import tpu as pltpu
from jax.sharding import PartitionSpec as P

f32 = jnp.float32
bf16 = jnp.bfloat16
NN = (((1,), (0,)), ((), ()))
NT = (((1,), (1,)), ((), ()))
TN = (((0,), (0,)), ((), ()))
LOG2E = 1.4426950408889634
ALL = slice(None)


def split(x):
    hi = x.astype(bf16)
    return hi, (x - hi.astype(f32)).astype(bf16)


def mm(a, b, dims):
    return lax.dot_general(a, b, dims, preferred_element_type=f32)


def mm3(a, b, dims):
    ah, al = split(a)
    bh, bl = split(b)
    return mm(ah, bh, dims) + (mm(ah, bl, dims) + mm(al, bh, dims))


def fit(fun, deg, lim):
    k = np.arange(200)
    z = 0.5 * lim * (1 - np.cos(np.pi * (k + 0.5) / 200))
    ch = np.polynomial.chebyshev.Chebyshev.fit(z, fun(z), deg, domain=[0, lim])
    return [float(v) for v in ch.convert(kind=np.polynomial.Polynomial).coef]


S_C = fit(lambda z: math.sqrt(2.0) * np.sinc(np.sqrt(z)) * np.pi, 4, 0.25)
C_C = fit(lambda z: math.sqrt(2.0) * np.cos(np.pi * np.sqrt(z)), 4, 0.25)


def sincos(u):
    r = u - jnp.round(u)
    z = r * r
    s = S_C[3] + S_C[4] * z
    c = C_C[3] + C_C[4] * z
    for i in (2, 1, 0):
        s = s * z + S_C[i]
        c = c * z + C_C[i]
    s = s * r
    return 1.0 - s * s, s * c


def phase_operand(pos, cell0):
    rows = []
    for d, n in enumerate((16.0, 8.0, 8.0)):
        parts = []
        for p in range(4):
            off = (p // 2, p % 2, 0)[d]
            parts.append((pos[p // 2, p % 2, d] + (cell0[d] + off).astype(f32)) * (1.0 / n))
        v = jnp.concatenate(parts, axis=1)
        a = v.astype(bf16)
        v = v - a.astype(f32)
        b = v.astype(bf16)
        v = v - b.astype(f32)
        rows += [a, b, v.astype(bf16)]
    rows.append(jnp.zeros((7, 512), bf16))
    return jnp.concatenate(rows, axis=0)


def wave_operand(waves, w16):
    w = waves[...].astype(f32)
    w16[...] = jnp.concatenate(
        [w[d:d + 1] for d in range(3) for _ in range(3)] + [jnp.zeros((7, 2048), f32)], axis=0).astype(bf16)


IC = 32


def own_positions(H, PI, p):
    for d in range(3):
        row = H[1 + p // 2, 1 + p % 2, 1, 128 + d:129 + d, :]
        PI[p, d] = jnp.broadcast_to(row, (128, 128)).T


OWN_CELLS = [(x, y, 1) for x in (1, 2) for y in (1, 2)] + [(x, y, z) for x in (1, 2) for y in (1, 2) for z in (0, 2)]


def make_vb(H, dst, at, x, y, z):
    hi, lo = split(H[x, y, z, 0:128, :])
    dst[at + (ALL, slice(0, 128))] = hi
    dst[at + (ALL, slice(128, 256))] = lo


def build(H, own, K, n, cell, shift, i0, is_self):
    x, y, z = cell
    r2 = None
    for d in range(3):
        row = H[x, y, z, 128 + d:129 + d, :] + shift[d]
        u = row - own[d]
        r2 = u * u if r2 is None else r2 + u * u
    e = jnp.maximum(1.0 - r2, 0.0)
    e = e * e
    if is_self is not None:
        ii = lax.broadcasted_iota(jnp.int32, (IC, 128), 0) + (i0 + jnp.where(is_self, 0, 1024))
        jj = lax.broadcasted_iota(jnp.int32, (IC, 128), 1)
        e = jnp.where(ii == jj, 0.0, e)
    rc = jnp.maximum(r2, 1e-30)
    w = jnp.exp2((rc * lax.rsqrt(rc)) * (14.0 * LOG2E))
    h = jnp.exp2(r2 * (-49.0 * LOG2E)) * e
    cols = slice(n * 128, (n + 1) * 128)
    for k in range(8):
        hi, lo = split(h)
        K[k * IC:(k + 1) * IC, cols] = hi
        K[(k + 8) * IC:(k + 9) * IC, cols] = lo
        if k < 7:
            h = h * w


def pair_unit(H, PI, va, vy, vb, K, mix, msg, t, phase):
    p = t // (128 // IC)
    ic = t % (128 // IC)
    px, py = p // 2, p % 2
    i0 = pl.multiple_of(ic * IC, IC)
    own = [PI[p, d, pl.ds(i0, IC), :] for d in range(3)]
    if phase == 0:
        runs = [OWN_CELLS[0:4]]
    elif phase == 1:
        runs = [OWN_CELLS[4:12]]
    elif phase == 2:
        runs = [[(x, 3 * py, z) for x in (1, 2) for z in range(3)]]
    else:
        runs = [[(3 * px, py + b, z) for b in range(3) for z in range(3)]]
    n = 0
    acc = None
    for run in runs:
        first = n
        for cell in run:
            x, y, z = cell
            shift = [jnp.asarray(x - 1 - px).astype(f32), jnp.asarray(y - 1 - py).astype(f32), z - 1.0]
            is_self = (p == (x - 1) * 2 + (y - 1)) if phase == 0 else None
            build(H, own, K, n, cell, shift, i0, is_self)
            n += 1
        x, y, _ = run[0]
        if phase < 2:
            v = va[4 * phase:4 * phase + len(run)].reshape(128 * len(run), 256)
        elif phase == 2:
            v = vy[py].reshape(768, 256)
        else:
            v = vb[px, pl.ds(y, 3)].reshape(1152, 256)
        t_ = mm(K[:, first * 128:n * 128], v, NN)
        acc = t_ if acc is None else acc + t_
    out = None
    for k in range(8):
        hh = acc[k * IC:(k + 1) * IC, :]
        s = (hh[:, 0:128] + (hh[:, 128:256] + acc[(k + 8) * IC:(k + 9) * IC, 0:128])) * mix[k:k + 1, :]
        out = s if out is None else out + s
    rows = pl.ds(i0, IC)
    if phase == 0:
        msg[p, rows, :] = out
    else:
        msg[p, rows, :] = msg[p, rows, :] + out


MESH_ID = pl.DeviceIdType.MESH
FILTER_SCALE = 1.0 / math.sqrt(131072.0) / math.sqrt(2048.0)


class Place:
    def __init__(self):
        self.gx = lax.axis_index("gx")
        self.gy = lax.axis_index("gy")
        self.gz = lax.axis_index("gz")
        self.core = self.gx % 2
        self.zh = self.gx // 2
        self.x = self.gy
        self.y = self.gz // 2
        self.zl = self.gz % 2
        self.z = self.zh * 2 + self.zl

    def at_gx(self, v):
        return (v, self.gy, self.gz)

    def at_gy(self, v):
        return (self.gx, v, self.gz)

    def at_gz(self, v):
        return (self.gx, self.gy, v)

    def at_y(self, v):
        return (self.gx, self.gy, v * 2 + self.zl)

    def at_z(self, v):
        return (v // 2 * 2 + self.core, self.gy, self.y * 2 + v % 2)


def flip(v, bits):
    if bits == 1:
        return v + 1 - 2 * (v % 2)
    if bits == 3:
        return 3 - v
    return (v + 2) % 4


class Copies:
    def __init__(self, send, recv):
        self.send, self.recv, self.n, self.started = send, recv, 0, []

    def start(self, src, dst, device):
        i = self.n
        self.n += 1
        cp = pltpu.make_async_remote_copy(
            src_ref=src, dst_ref=dst, send_sem=self.send.at[i], recv_sem=self.recv.at[i],
            device_id=device, device_id_type=MESH_ID)
        cp.start()
        self.started.append(cp)
        return cp

    def finish(self):
        for cp in self.started:
            cp.wait_send()


def greet(me):
    bar = pltpu.get_barrier_semaphore()
    peers = [me.at_gx((me.gx + 1) % 8), me.at_gx((me.gx + 7) % 8),
             me.at_gy((me.gy + 1) % 4), me.at_gy((me.gy + 3) % 4),
             me.at_gz((me.gz + 2) % 8), me.at_gz((me.gz + 6) % 8),
             me.at_gy((me.gy + 2) % 4), me.at_gz((me.gz + 4) % 8)]
    peers += [me.at_z((me.z + i) % 8) for i in range(1, 8)]
    for p in peers:
        pl.semaphore_signal(bar, inc=1, device_id=p, device_id_type=MESH_ID)
    return lambda: pl.semaphore_wait(bar, len(peers))


def halo_steps(me, cp, H):
    st = {}
    up_y, down_y = me.at_gy((me.gy + 1) % 4), me.at_gy((me.gy + 3) % 4)
    up_x, down_x = me.at_gx((me.gx + 1) % 8), me.at_gx((me.gx + 7) % 8)

    def h0():
        st["pair"] = [cp.start(H.at[1 + p // 2, 1 + p % 2, 1], H.at[1 + p // 2, 1 + p % 2, 2 * me.zl],
                               me.at_gz(me.gz + 1 - 2 * me.zl)) for p in range(4)]
        st["gy"] = [cp.start(H.at[1:3, 2, 1], H.at[1:3, 0, 1], up_y),
                    cp.start(H.at[1:3, 1, 1], H.at[1:3, 3, 1], down_y)]

    def h1():
        st["fwd"] = []
        for p in range(4):
            st["pair"][p].wait_recv()
            c = (1 + p // 2, 1 + p % 2)
            st["fwd"].append(cp.start(H.at[c[0], c[1], 2 - 2 * me.zl], H.at[c[0], c[1], 2 * me.zl],
                                      me.at_gz((me.gz + 2 + 4 * me.zl) % 8)))

    def h2():
        for c in st["fwd"]:
            c.wait_recv()
        st["gx"] = [cp.start(H.at[1 + me.core, 1:3], H.at[3 - 3 * me.core, 1:3], me.at_gx((me.gx + 7 + 2 * me.core) % 8)),
                    cp.start(H.at[2 - me.core, 1:3], H.at[3 * me.core, 1:3], me.at_gx(me.gx + 1 - 2 * me.core))]

    def h3():
        for z in (0, 2):
            st["gy"].append(cp.start(H.at[1:3, 2, z], H.at[1:3, 0, z], up_y))
            st["gy"].append(cp.start(H.at[1:3, 1, z], H.at[1:3, 3, z], down_y))

    def h4():
        for c in st["gx"]:
            c.wait_recv()
        far = 3 * me.core
        st["corner"] = [cp.start(H.at[far, 2], H.at[far, 0], up_y), cp.start(H.at[far, 1], H.at[far, 3], down_y)]

    def h5():
        for c in st["gy"]:
            c.wait_recv()
        for y in (0, 3):
            st["corner"].append(cp.start(H.at[2 - me.core, y], H.at[3 * me.core, y], me.at_gx(me.gx + 1 - 2 * me.core)))

    def h6():
        for c in st["corner"]:
            c.wait_recv()
    return [h0, h1, h2, h3, h4, h5, h6]


def core_copy(me, F, RD, dsem, i):
    rows = pl.ds(pl.multiple_of(64 - me.core * 64, 64), 64)
    return pltpu.make_async_remote_copy(
        src_ref=F.at[i // 4, i % 4, :, rows], dst_ref=RD.at[i // 4, i % 4],
        send_sem=dsem.at[0, i], recv_sem=dsem.at[1, i],
        device_id=me.at_gx(me.gx + 1 - 2 * me.core), device_id_type=MESH_ID)


def reduce_steps(me, cp, Fs, Gs, Rs, dsem, filt, h):
    F, G = Fs.at[h], Gs.at[h]
    RD, R1, R2, R3, RZ = [r.at[h] for r in Rs]
    c64 = me.core * 64
    other = me.at_gx(me.gx + 1 - 2 * me.core)
    st = {}
    groups = []
    for g in range(4):
        bits = (1, 3) if g % 2 == 0 else (3, 1)
        rows = pl.ds(pl.multiple_of(c64 + 16 * g, 16), 16)
        axes = [(me.y, me.at_y), (me.x, me.at_gy)]
        if g >= 2:
            axes = axes[::-1]

        def view(ref, first, second, rows=rows, g=g):
            return ref.at[first, second, rows] if g < 2 else ref.at[second, first, rows]
        groups.append((g, bits, rows, axes, view))

    def r1():
        for i in range(4 * h, 4 * h + 4):
            core_copy(me, Fs, Rs[0], dsem, i).wait_recv()
        for g, bits, rows, axes, view in groups:
            F[:, :, rows] = F[:, :, rows] + RD[:, :, 16 * g:16 * g + 16]
            v, at = axes[0]
            dev = at(flip(v, bits[0]))
            st["1", g] = [cp.start(view(F, flip(v, bits[0]), ALL), R1.at[g, 0], dev),
                          cp.start(view(F, flip(v, 2), ALL), R1.at[g, 1], dev)]

    def add(ref, first, second, val, g, rows):
        if g < 2:
            ref[first, second, rows] = ref[first, second, rows] + val
        else:
            ref[second, first, rows] = ref[second, first, rows] + val

    def r2():
        for g, bits, rows, axes, view in groups:
            v, at = axes[0]
            keep = (v, flip(v, bits[1]))
            for i in (1, 0):
                st["1", g][i].wait_recv()
                add(F, keep[i], ALL, R1[g, i], g, rows)
            st["2", g] = cp.start(view(F, keep[1], ALL), R2.at[g], at(flip(v, bits[1])))

    def r3():
        for g, bits, rows, axes, view in groups:
            v, at = axes[0]
            st["2", g].wait_recv()
            add(F, v, ALL, R2[g], g, rows)
            u, at = axes[1]
            st["3", g] = [cp.start(view(F, v, (u + i) % 4), R3.at[g, i - 1], at((u + i) % 4)) for i in (2, 1, 3)]

    def zrows(z):
        return pl.ds(pl.multiple_of(c64 + 8 * z, 8), 8)

    def r4():
        for g, bits, rows, axes, view in groups:
            for c in st["3", g]:
                c.wait_recv()
            add(F, axes[0][0], axes[1][0], R3[g, 0] + (R3[g, 1] + R3[g, 2]), g, rows)
        for i in (4, 3, 5, 2, 6, 1, 7):
            z = (me.z + i) % 8
            st["z", i] = cp.start(F.at[me.y, me.x, zrows(z)], RZ.at[i], me.at_z(z))

    def r5():
        total = F[me.y, me.x, zrows(me.z)]
        for i in (1, 7, 2, 6, 3, 5, 4):
            st["z", i].wait_recv()
            total = total + RZ[i]
        G[me.y, me.x, zrows(me.z)] = total * filt()
        for i in (4, 3, 5, 2, 6, 1, 7):
            mine = G.at[me.y, me.x, zrows(me.z)]
            st["Z", i] = cp.start(mine, mine, me.at_z((me.z + i) % 8))

    def same(ref, dev):
        return cp.start(ref, ref, dev)

    def r6():
        for i in range(1, 8):
            st["Z", i].wait_recv()
        for g, bits, rows, axes, view in groups:
            u, at = axes[1]
            st["3b", g] = [same(view(G, axes[0][0], u), at((u + i) % 4)) for i in (2, 1, 3)]

    def r7():
        for g, bits, rows, axes, view in groups:
            v, at = axes[0]
            for c in st["3b", g]:
                c.wait_recv()
            st["2b", g] = same(view(G, v, ALL), at(flip(v, bits[1])))

    def r8():
        st["Db"] = []
        for g, bits, rows, axes, view in groups:
            v, at = axes[0]
            st["2b", g].wait_recv()
            dev = at(flip(v, bits[0]))
            st["1b", g] = [same(view(G, v, ALL), dev), same(view(G, flip(v, bits[1]), ALL), dev)]
        for g, bits, rows, axes, view in groups:
            v = axes[0][0]
            for s in (v, flip(v, bits[1])):
                st["Db"].append(same(view(G, s, ALL), other))

    def r9():
        for g, bits, rows, axes, view in groups:
            v = axes[0][0]
            for c in st["1b", g]:
                c.wait_recv()
            for s in (flip(v, bits[0]), flip(v, 2)):
                st["Db"].append(same(view(G, s, ALL), other))

    def r10():
        for c in st["Db"]:
            c.wait_recv()
    return [None, r1, r2, r3, r4, r5, r6, r7, r8, r9, r10]


EVENTS = [
    "f46", "r01", "f68", "r11", "ca", "a4", "h1", "r02", "a4", "r12", "a4", "h2", "cA", "r03", "A1", "r13",
    "h3", "a4", "r04", "A3", "r14", "A3", "h4", "r05", "A4", "h5", "cB", "B1", "r15", "A3", "B3", "r06", "B4",
    "A2", "r16", "B4", "r07", "h6", "cC", "B4", "r17", "C3", "r08", "C3", "r18", "C3", "r09", "C3", "r19",
    "C3", "r010", "p0", "C1", "r110", "p1",
]


def parse(events):
    for w in events:
        if w[0] == "r":
            yield "r", int(w[1]), int(w[2:])
        elif w[0] == "f":
            yield "factors", int(w[1]), int(w[2])
        elif w[0] == "p":
            yield "pot", int(w[1])
        elif w[0] == "c":
            yield (w,)
        else:
            yield {"h": "h", "a": 0, "A": 1, "B": 2, "C": 3}[w[0]], int(w[1:])


PLAN = list(parse(EVENTS))


def kernel(feat, pos, counts, waves, filt_hbm, wv, wc, mix, wh, wo, out,
           H, F, G, RD, R1, R2, R3, RZ, TH, TL, q2, w16, fbuf, ftr, va, vy, vb, PI, K, m8, msg, potr,
           send, recv, dsem, lsem):
    me = Place()
    fcopy = [pltpu.make_async_copy(
        filt_hbm.at[pl.ds(pl.multiple_of((4 * h + me.y) * 256 + (me.x % 2) * 128, 128), 128)], fbuf.at[h], lsem.at[h])
        for h in range(2)]
    for c in fcopy:
        c.start()
    greeted = greet(me)
    lane = lax.broadcasted_iota(jnp.int32, (128, 128), 1)
    sub = lax.broadcasted_iota(jnp.int32, (128, 128), 0)
    cells = [(p // 2, p % 2, 0) for p in range(4)]
    for p, c in enumerate(cells):
        q = jnp.where(lane < counts[c[0], 0, c[1]], mm3(wc[...], feat[c], TN), 0.0)
        hi, lo = split(q)
        q2[0:128, p * 128:(p + 1) * 128] = hi
        q2[128:256, p * 128:(p + 1) * 128] = lo
        v = mm3(feat[c], wv[...], TN)
        H[1 + c[0], 1 + c[1], 1, 0:128, :] = jnp.where(sub < counts[c[0], 0, c[1]], v, 0.0)
        H[1 + c[0], 1 + c[1], 1, 128:136, :] = jnp.concatenate(
            [pos[c[0], c[1], d] for d in range(3)] + [jnp.zeros((5, 128), f32)], axis=0)
    wave_operand(waves, w16)
    fr = phase_operand(pos, (me.gx * 2, me.gy * 2, me.gz))

    def factors(i, send_now):
        u = mm(w16[:, pl.ds(pl.multiple_of(i * 256, 256), 256)], fr, TN)
        c, s = sincos(u)
        for t, k, x in ((c, i, 0), (s, i + 8, 2)):
            th, tl = split(t)
            TH[k] = th
            TL[k] = tl
            big = mm(q2[...], th, NT)
            f = big[0:128] + (big[128:256] + mm(q2[0:128], tl, NT))
            F[i // 4, i % 4, x] = f[:, 0:128]
            F[i // 4, i % 4, x + 1] = f[:, 128:256]
        if send_now:
            core_copy(me, F, RD, dsem, i).start()

    def factor_loop(lo, hi, send_now):
        def body(i, _):
            factors(i, send_now)
            return 0
        lax.fori_loop(lo, hi, body, 0)
    factor_loop(0, 4, False)
    for c in fcopy:
        c.wait()
    for h in range(2):
        ftr[h] = fbuf[h].T
    for k in range(8):
        m8[k:k + 1, :] = mix[k:k + 1, :] * math.exp(-float(k * k))
    for p in range(4):
        own_positions(H, PI, p)
    greeted()
    for i in range(4):
        core_copy(me, F, RD, dsem, i).start()
    cp = Copies(send, recv)
    hs = halo_steps(me, cp, H)
    hs[0]()

    def filt(h):
        return lambda: ftr[h, pl.ds(pl.multiple_of(me.core * 64 + 8 * me.z, 8), 8), :] * FILTER_SCALE

    rs = [reduce_steps(me, cp, F, G, (RD, R1, R2, R3, RZ), dsem, filt(h), h) for h in range(2)]

    def convert(dst, at_of, cells_of, n):
        def body(i, _):
            make_vb(H, dst, at_of(i), *cells_of(i))
            return 0
        lax.fori_loop(0, n, body, 0)

    def potential(h):
        def body(j, acc):
            y, t = j // 2, j % 2
            g = jnp.concatenate([G[h, y, 2 * t], G[h, y, 2 * t + 1]], axis=1)
            gh, gl = split(g)
            k = 4 * h + y + 8 * t
            big = mm(jnp.concatenate([gh, gl], axis=0), TH[k], NN)
            return acc + (big[0:128] + (big[128:256] + mm(gh, TL[k], NN)))
        potr[...] = lax.fori_loop(0, 8, body, potr[...] if h else jnp.zeros((128, 512), f32))

    at = [0, 0, 0, 0]
    for item in PLAN:
        if item[0] == "h":
            hs[item[1]]()
        elif item[0] == "r":
            rs[item[1]][item[2]]()
        elif item[0] == "factors":
            factor_loop(item[1], item[2], True)
        elif item[0] == "pot":
            potential(item[1])
        elif item[0] == "ca":
            for n in range(4):
                make_vb(H, va, (n,), *OWN_CELLS[n])
        elif item[0] == "cA":
            for n in range(4, 12):
                make_vb(H, va, (n,), *OWN_CELLS[n])
        elif item[0] == "cB":
            convert(vy, lambda i: (i // 6, (i // 3) % 2, i % 3), lambda i: (1 + (i // 3) % 2, 3 * (i // 6), i % 3), 12)
        elif item[0] == "cC":
            convert(vb, lambda i: (i // 12, (i // 3) % 4, i % 3), lambda i: (3 * (i // 12), (i // 3) % 4, i % 3), 24)
        else:
            def body(t, _, phase=item[0]):
                pair_unit(H, PI, va, vy, vb, K, m8, msg, t, phase)
                return 0
            lax.fori_loop(at[item[0]], at[item[0]] + item[1], body, 0)
            at[item[0]] += item[1]

    for p, c in enumerate(cells):
        mixed = feat[c] + 0.125 * msg[p].T + potr[:, p * 128:(p + 1) * 128]
        h = mm3(wh[...], mixed, TN)
        h = h / (1.0 + jnp.exp(-h))
        o = mixed + mm3(wo[...], h, TN)
        out[c] = jnp.where(lane < counts[c[0], 0, c[1]], o, 0.0)
    cp.finish()
    for i in range(8):
        core_copy(me, F, RD, dsem, i).wait_send()


NCOPY = 176


def shards(features, positions, counts, waves, filter_table, w_value, w_charge, radial_mix, w_hidden, w_out):
    V = pl.BlockSpec(memory_space=pltpu.VMEM)
    S = pl.BlockSpec(memory_space=pltpu.SMEM)
    A = pl.BlockSpec(memory_space=pl.ANY)
    vm = pltpu.VMEM
    return pl.pallas_call(
        kernel,
        out_shape=jax.ShapeDtypeStruct(features.shape, f32),
        in_specs=[V, V, S, V, A, V, V, V, V, V], out_specs=V,
        scratch_shapes=[
            vm((4, 4, 3, 136, 128), f32), vm((2, 4, 4, 128, 128), f32), vm((2, 4, 4, 128, 128), f32),
            vm((2, 4, 4, 64, 128), f32), vm((2, 4, 2, 4, 16, 128), f32),
            vm((2, 4, 4, 16, 128), f32), vm((2, 4, 3, 16, 128), f32),
            vm((2, 8, 8, 128), f32),
            vm((16, 256, 512), bf16), vm((16, 256, 512), bf16), vm((256, 512), bf16), vm((16, 2048), bf16),
            vm((2, 128, 128), f32), vm((2, 128, 128), f32),
            vm((12, 128, 256), bf16), vm((2, 2, 3, 128, 256), bf16), vm((2, 4, 3, 128, 256), bf16), vm((4, 3, 128, 128), f32),
            vm((16 * IC, 1152), bf16), vm((8, 128), f32), vm((4, 128, 128), f32), vm((128, 512), f32),
            pltpu.SemaphoreType.DMA((NCOPY,)), pltpu.SemaphoreType.DMA((NCOPY,)),
            pltpu.SemaphoreType.DMA((2, 8)), pltpu.SemaphoreType.DMA((2,)),
        ],
        compiler_params=pltpu.CompilerParams(collective_id=0, has_side_effects=True),
        name="layer",
    )(features, positions.reshape(2, 2, 3, 1, 128), counts.reshape(2, 1, 2), waves, filter_table,
      w_value, w_charge, radial_mix, w_hidden, w_out)


def solution(mesh):
    cell = P("gx", "gy", "gz")
    five = P("gx", "gy", "gz", None, None)
    return jax.shard_map(
        shards, mesh=mesh,
        in_specs=(five, five, cell) + (P(),) * 7,
        out_specs=five, check_vma=False)
```

```python
import math
import functools
import jax, jax.numpy as jnp, numpy as np
from jax import lax
from jax.experimental import pallas as pl
from jax.experimental.pallas import tpu as pltpu
from jax.sharding import PartitionSpec as P

f32 = jnp.float32
bf16 = jnp.bfloat16
NN = (((1,), (0,)), ((), ()))
NT = (((1,), (1,)), ((), ()))
TN = (((0,), (0,)), ((), ()))
LOG2E = 1.4426950408889634
ALL = slice(None)


def split(x):
    hi = x.astype(bf16)
    return hi, (x - hi.astype(f32)).astype(bf16)


def mm(a, b, dims):
    return lax.dot_general(a, b, dims, preferred_element_type=f32)


def mm3(a, b, dims):
    ah, al = split(a)
    bh, bl = split(b)
    return mm(ah, bh, dims) + (mm(ah, bl, dims) + mm(al, bh, dims))


def fit(fun, deg, lim):
    k = np.arange(200)
    z = 0.5 * lim * (1 - np.cos(np.pi * (k + 0.5) / 200))
    ch = np.polynomial.chebyshev.Chebyshev.fit(z, fun(z), deg, domain=[0, lim])
    return [float(v) for v in ch.convert(kind=np.polynomial.Polynomial).coef]


S_C = fit(lambda z: math.sqrt(2.0) * np.sinc(np.sqrt(z)) * np.pi, 4, 0.25)
C_C = fit(lambda z: math.sqrt(2.0) * np.cos(np.pi * np.sqrt(z)), 4, 0.25)


def sincos(u):
    r = u - jnp.round(u)
    z = r * r
    s = S_C[3] + S_C[4] * z
    c = C_C[3] + C_C[4] * z
    for i in (2, 1, 0):
        s = s * z + S_C[i]
        c = c * z + C_C[i]
    s = s * r
    return 1.0 - s * s, s * c


def phase_operand(pos, cell0):
    rows = []
    for d, n in enumerate((16.0, 8.0, 8.0)):
        parts = []
        for p in range(4):
            off = (p // 2, p % 2, 0)[d]
            parts.append((pos[p // 2, p % 2, d] + (cell0[d] + off).astype(f32)) * (1.0 / n))
        v = jnp.concatenate(parts, axis=1)
        a = v.astype(bf16)
        v = v - a.astype(f32)
        b = v.astype(bf16)
        v = v - b.astype(f32)
        rows += [a, b, v.astype(bf16)]
    rows.append(jnp.zeros((7, 512), bf16))
    return jnp.concatenate(rows, axis=0)


def wave_operand(waves, w16):
    w = waves[...].astype(f32)
    w16[...] = jnp.concatenate(
        [w[d:d + 1] for d in range(3) for _ in range(3)] + [jnp.zeros((7, 2048), f32)], axis=0).astype(bf16)


IC = 32


def own_positions(H, PI, p):
    for d in range(3):
        row = H[1 + p // 2, 1 + p % 2, 1, 128 + d:129 + d, :]
        PI[p, d] = jnp.broadcast_to(row, (128, 128)).T


OWN_CELLS = [(x, y, 1) for x in (1, 2) for y in (1, 2)] + [(x, y, z) for x in (1, 2) for y in (1, 2) for z in (0, 2)]


def make_vb(H, dst, at, x, y, z):
    hi, lo = split(H[x, y, z, 0:128, :])
    dst[at + (ALL, slice(0, 128))] = hi
    dst[at + (ALL, slice(128, 256))] = lo


def build(H, own, K, n, cell, shift, i0, is_self):
    x, y, z = cell
    r2 = None
    for d in range(3):
        row = H[x, y, z, 128 + d:129 + d, :] + shift[d]
        u = row - own[d]
        r2 = u * u if r2 is None else r2 + u * u
    e = jnp.maximum(1.0 - r2, 0.0)
    e = e * e
    if is_self is not None:
        ii = lax.broadcasted_iota(jnp.int32, (IC, 128), 0) + (i0 + jnp.where(is_self, 0, 1024))
        jj = lax.broadcasted_iota(jnp.int32, (IC, 128), 1)
        e = jnp.where(ii == jj, 0.0, e)
    rc = jnp.maximum(r2, 1e-30)
    w = jnp.exp2((rc * lax.rsqrt(rc)) * (14.0 * LOG2E))
    h = jnp.exp2(r2 * (-49.0 * LOG2E)) * e
    cols = slice(n * 128, (n + 1) * 128)
    for k in range(8):
        hi, lo = split(h)
        K[k * IC:(k + 1) * IC, cols] = hi
        K[(k + 8) * IC:(k + 9) * IC, cols] = lo
        if k < 7:
            h = h * w


def pair_unit(H, PI, va, vy, vb, K, mix, msg, t, phase):
    p = t // (128 // IC)
    ic = t % (128 // IC)
    px, py = p // 2, p % 2
    i0 = pl.multiple_of(ic * IC, IC)
    own = [PI[p, d, pl.ds(i0, IC), :] for d in range(3)]
    if phase == 0:
        runs = [OWN_CELLS[0:4]]
    elif phase == 1:
        runs = [OWN_CELLS[4:12]]
    elif phase == 2:
        runs = [[(x, 3 * py, z) for x in (1, 2) for z in range(3)]]
    else:
        runs = [[(3 * px, py + b, z) for b in range(3) for z in range(3)]]
    n = 0
    acc = None
    for run in runs:
        first = n
        for cell in run:
            x, y, z = cell
            shift = [jnp.asarray(x - 1 - px).astype(f32), jnp.asarray(y - 1 - py).astype(f32), z - 1.0]
            is_self = (p == (x - 1) * 2 + (y - 1)) if phase == 0 else None
            build(H, own, K, n, cell, shift, i0, is_self)
            n += 1
        x, y, _ = run[0]
        if phase < 2:
            v = va[4 * phase:4 * phase + len(run)].reshape(128 * len(run), 256)
        elif phase == 2:
            v = vy[py].reshape(768, 256)
        else:
            v = vb[px, pl.ds(y, 3)].reshape(1152, 256)
        t_ = mm(K[:, first * 128:n * 128], v, NN)
        acc = t_ if acc is None else acc + t_
    out = None
    for k in range(8):
        hh = acc[k * IC:(k + 1) * IC, :]
        s = (hh[:, 0:128] + (hh[:, 128:256] + acc[(k + 8) * IC:(k + 9) * IC, 0:128])) * mix[k:k + 1, :]
        out = s if out is None else out + s
    rows = pl.ds(i0, IC)
    if phase == 0:
        msg[p, rows, :] = out
    else:
        msg[p, rows, :] = msg[p, rows, :] + out


MESH_ID = pl.DeviceIdType.MESH
FILTER_SCALE = 1.0 / math.sqrt(131072.0) / math.sqrt(2048.0)


class Place:
    def __init__(self):
        self.gx = lax.axis_index("gx")
        self.gy = lax.axis_index("gy")
        self.gz = lax.axis_index("gz")
        self.core = self.gx % 2
        self.zh = self.gx // 2
        self.x = self.gy
        self.y = self.gz // 2
        self.zl = self.gz % 2
        self.z = self.zh * 2 + self.zl

    def at_gx(self, v):
        return (v, self.gy, self.gz)

    def at_gy(self, v):
        return (self.gx, v, self.gz)

    def at_gz(self, v):
        return (self.gx, self.gy, v)

    def at_y(self, v):
        return (self.gx, self.gy, v * 2 + self.zl)

    def at_z(self, v):
        return (v // 2 * 2 + self.core, self.gy, self.y * 2 + v % 2)


def flip(v, bits):
    if bits == 1:
        return v + 1 - 2 * (v % 2)
    if bits == 3:
        return 3 - v
    return (v + 2) % 4


class Copies:
    def __init__(self, send, recv):
        self.send, self.recv, self.n, self.started = send, recv, 0, []

    def start(self, src, dst, device):
        i = self.n
        self.n += 1
        cp = pltpu.make_async_remote_copy(
            src_ref=src, dst_ref=dst, send_sem=self.send.at[i], recv_sem=self.recv.at[i],
            device_id=device, device_id_type=MESH_ID)
        cp.start()
        self.started.append(cp)
        return cp

    def finish(self):
        for cp in self.started:
            cp.wait_send()


def greet(me):
    bar = pltpu.get_barrier_semaphore()
    peers = [me.at_gx((me.gx + 1) % 8), me.at_gx((me.gx + 7) % 8),
             me.at_gy((me.gy + 1) % 4), me.at_gy((me.gy + 3) % 4),
             me.at_gz((me.gz + 2) % 8), me.at_gz((me.gz + 6) % 8),
             me.at_gy((me.gy + 2) % 4), me.at_gz((me.gz + 4) % 8)]
    peers += [me.at_z((me.z + i) % 8) for i in range(1, 8)]
    for p in peers:
        pl.semaphore_signal(bar, inc=1, device_id=p, device_id_type=MESH_ID)
    return lambda: pl.semaphore_wait(bar, len(peers))


def halo_steps(me, cp, H):
    st = {}
    up_y, down_y = me.at_gy((me.gy + 1) % 4), me.at_gy((me.gy + 3) % 4)
    up_x, down_x = me.at_gx((me.gx + 1) % 8), me.at_gx((me.gx + 7) % 8)

    def h0():
        st["pair"] = [cp.start(H.at[1 + p // 2, 1 + p % 2, 1], H.at[1 + p // 2, 1 + p % 2, 2 * me.zl],
                               me.at_gz(me.gz + 1 - 2 * me.zl)) for p in range(4)]
        st["gy"] = [cp.start(H.at[1:3, 2, 1], H.at[1:3, 0, 1], up_y),
                    cp.start(H.at[1:3, 1, 1], H.at[1:3, 3, 1], down_y)]

    def h1():
        st["fwd"] = []
        for p in range(4):
            st["pair"][p].wait_recv()
            c = (1 + p // 2, 1 + p % 2)
            st["fwd"].append(cp.start(H.at[c[0], c[1], 2 - 2 * me.zl], H.at[c[0], c[1], 2 * me.zl],
                                      me.at_gz((me.gz + 2 + 4 * me.zl) % 8)))

    def h2():
        for c in st["fwd"]:
            c.wait_recv()
        st["gx"] = [cp.start(H.at[1 + me.core, 1:3], H.at[3 - 3 * me.core, 1:3], me.at_gx((me.gx + 7 + 2 * me.core) % 8)),
                    cp.start(H.at[2 - me.core, 1:3], H.at[3 * me.core, 1:3], me.at_gx(me.gx + 1 - 2 * me.core))]

    def h3():
        for z in (0, 2):
            st["gy"].append(cp.start(H.at[1:3, 2, z], H.at[1:3, 0, z], up_y))
            st["gy"].append(cp.start(H.at[1:3, 1, z], H.at[1:3, 3, z], down_y))

    def h4():
        for c in st["gx"]:
            c.wait_recv()
        far = 3 * me.core
        st["corner"] = [cp.start(H.at[far, 2], H.at[far, 0], up_y), cp.start(H.at[far, 1], H.at[far, 3], down_y)]

    def h5():
        for c in st["gy"]:
            c.wait_recv()
        for y in (0, 3):
            st["corner"].append(cp.start(H.at[2 - me.core, y], H.at[3 * me.core, y], me.at_gx(me.gx + 1 - 2 * me.core)))

    def h6():
        for c in st["corner"]:
            c.wait_recv()
    return [h0, h1, h2, h3, h4, h5, h6]


def core_copy(me, F, RD, dsem, i):
    rows = pl.ds(pl.multiple_of(64 - me.core * 64, 64), 64)
    return pltpu.make_async_remote_copy(
        src_ref=F.at[i // 4, i % 4, :, rows], dst_ref=RD.at[i // 4, i % 4],
        send_sem=dsem.at[0, i], recv_sem=dsem.at[1, i],
        device_id=me.at_gx(me.gx + 1 - 2 * me.core), device_id_type=MESH_ID)


def reduce_steps(me, cp, Fs, Gs, Rs, dsem, filt, h):
    F, G = Fs.at[h], Gs.at[h]
    RD, R1, R2, R3, RZ = [r.at[h] for r in Rs]
    c64 = me.core * 64
    other = me.at_gx(me.gx + 1 - 2 * me.core)
    st = {}
    groups = []
    for g in range(4):
        bits = (1, 3) if g % 2 == 0 else (3, 1)
        rows = pl.ds(pl.multiple_of(c64 + 16 * g, 16), 16)
        axes = [(me.y, me.at_y), (me.x, me.at_gy)]
        if g >= 2:
            axes = axes[::-1]

        def view(ref, first, second, rows=rows, g=g):
            return ref.at[first, second, rows] if g < 2 else ref.at[second, first, rows]
        groups.append((g, bits, rows, axes, view))

    def r1():
        for i in range(4 * h, 4 * h + 4):
            core_copy(me, Fs, Rs[0], dsem, i).wait_recv()
        for g, bits, rows, axes, view in groups:
            F[:, :, rows] = F[:, :, rows] + RD[:, :, 16 * g:16 * g + 16]
            v, at = axes[0]
            dev = at(flip(v, bits[0]))
            st["1", g] = [cp.start(view(F, flip(v, bits[0]), ALL), R1.at[g, 0], dev),
                          cp.start(view(F, flip(v, 2), ALL), R1.at[g, 1], dev)]

    def add(ref, first, second, val, g, rows):
        if g < 2:
            ref[first, second, rows] = ref[first, second, rows] + val
        else:
            ref[second, first, rows] = ref[second, first, rows] + val

    def r2():
        for g, bits, rows, axes, view in groups:
            v, at = axes[0]
            keep = (v, flip(v, bits[1]))
            for i in (1, 0):
                st["1", g][i].wait_recv()
                add(F, keep[i], ALL, R1[g, i], g, rows)
            st["2", g] = cp.start(view(F, keep[1], ALL), R2.at[g], at(flip(v, bits[1])))

    def r3():
        for g, bits, rows, axes, view in groups:
            v, at = axes[0]
            st["2", g].wait_recv()
            add(F, v, ALL, R2[g], g, rows)
            u, at = axes[1]
            st["3", g] = [cp.start(view(F, v, (u + i) % 4), R3.at[g, i - 1], at((u + i) % 4)) for i in (2, 1, 3)]

    def zrows(z):
        return pl.ds(pl.multiple_of(c64 + 8 * z, 8), 8)

    def r4():
        for g, bits, rows, axes, view in groups:
            for c in st["3", g]:
                c.wait_recv()
            add(F, axes[0][0], axes[1][0], R3[g, 0] + (R3[g, 1] + R3[g, 2]), g, rows)
        for i in (4, 3, 5, 2, 6, 1, 7):
            z = (me.z + i) % 8
            st["z", i] = cp.start(F.at[me.y, me.x, zrows(z)], RZ.at[i], me.at_z(z))

    def r5():
        total = F[me.y, me.x, zrows(me.z)]
        for i in (1, 7, 2, 6, 3, 5, 4):
            st["z", i].wait_recv()
            total = total + RZ[i]
        G[me.y, me.x, zrows(me.z)] = total * filt()
        for i in (4, 3, 5, 2, 6, 1, 7):
            mine = G.at[me.y, me.x, zrows(me.z)]
            st["Z", i] = cp.start(mine, mine, me.at_z((me.z + i) % 8))

    def same(ref, dev):
        return cp.start(ref, ref, dev)

    def r6():
        for i in range(1, 8):
            st["Z", i].wait_recv()
        for g, bits, rows, axes, view in groups:
            u, at = axes[1]
            st["3b", g] = [same(view(G, axes[0][0], u), at((u + i) % 4)) for i in (2, 1, 3)]

    def r7():
        for g, bits, rows, axes, view in groups:
            v, at = axes[0]
            for c in st["3b", g]:
                c.wait_recv()
            st["2b", g] = same(view(G, v, ALL), at(flip(v, bits[1])))

    def r8():
        st["Db"] = []
        for g, bits, rows, axes, view in groups:
            v, at = axes[0]
            st["2b", g].wait_recv()
            dev = at(flip(v, bits[0]))
            st["1b", g] = [same(view(G, v, ALL), dev), same(view(G, flip(v, bits[1]), ALL), dev)]
        for g, bits, rows, axes, view in groups:
            v = axes[0][0]
            for s in (v, flip(v, bits[1])):
                st["Db"].append(same(view(G, s, ALL), other))

    def r9():
        for g, bits, rows, axes, view in groups:
            v = axes[0][0]
            for c in st["1b", g]:
                c.wait_recv()
            for s in (flip(v, bits[0]), flip(v, 2)):
                st["Db"].append(same(view(G, s, ALL), other))

    def r10():
        for c in st["Db"]:
            c.wait_recv()
    return [None, r1, r2, r3, r4, r5, r6, r7, r8, r9, r10]


EVENTS = [
    "f46", "r01", "f68", "r11", "ca", "a4", "h1", "r02", "a4", "r12", "a4", "h2", "cA", "r03", "A1", "r13",
    "h3", "a4", "r04", "A3", "r14", "A3", "h4", "r05", "A4", "h5", "cB", "B1", "r15", "A3", "B3", "r06", "B4",
    "A2", "r16", "B4", "r07", "h6", "cC", "B4", "r17", "C4", "r08", "C3", "r18", "C3", "r09", "C3", "r19",
    "C3", "r010", "p0", "r110", "p1",
]


def parse(events):
    for w in events:
        if w[0] == "r":
            yield "r", int(w[1]), int(w[2:])
        elif w[0] == "f":
            yield "factors", int(w[1]), int(w[2])
        elif w[0] == "p":
            yield "pot", int(w[1])
        elif w[0] == "c":
            yield (w,)
        else:
            yield {"h": "h", "a": 0, "A": 1, "B": 2, "C": 3}[w[0]], int(w[1:])


PLAN = list(parse(EVENTS))


def kernel(feat, pos, counts, waves, filt_hbm, wv, wc, mix, wh, wo, out,
           H, F, G, RD, R1, R2, R3, RZ, TH, TL, q2, w16, fbuf, ftr, va, vy, vb, PI, K, m8, msg, potr,
           send, recv, dsem, lsem):
    me = Place()
    fcopy = [pltpu.make_async_copy(
        filt_hbm.at[pl.ds(pl.multiple_of((4 * h + me.y) * 256 + (me.x % 2) * 128, 128), 128)], fbuf.at[h], lsem.at[h])
        for h in range(2)]
    for c in fcopy:
        c.start()
    greeted = greet(me)
    lane = lax.broadcasted_iota(jnp.int32, (128, 128), 1)
    sub = lax.broadcasted_iota(jnp.int32, (128, 128), 0)
    cells = [(p // 2, p % 2, 0) for p in range(4)]
    for p, c in enumerate(cells):
        q = jnp.where(lane < counts[c[0], 0, c[1]], mm3(wc[...], feat[c], TN), 0.0)
        hi, lo = split(q)
        q2[0:128, p * 128:(p + 1) * 128] = hi
        q2[128:256, p * 128:(p + 1) * 128] = lo
        v = mm3(feat[c], wv[...], TN)
        H[1 + c[0], 1 + c[1], 1, 0:128, :] = jnp.where(sub < counts[c[0], 0, c[1]], v, 0.0)
        H[1 + c[0], 1 + c[1], 1, 128:136, :] = jnp.concatenate(
            [pos[c[0], c[1], d] for d in range(3)] + [jnp.zeros((5, 128), f32)], axis=0)
    wave_operand(waves, w16)
    fr = phase_operand(pos, (me.gx * 2, me.gy * 2, me.gz))

    def factors(i, send_now):
        u = mm(w16[:, pl.ds(pl.multiple_of(i * 256, 256), 256)], fr, TN)
        c, s = sincos(u)
        for t, k, x in ((c, i, 0), (s, i + 8, 2)):
            th, tl = split(t)
            TH[k] = th
            TL[k] = tl
            big = mm(q2[...], th, NT)
            f = big[0:128] + (big[128:256] + mm(q2[0:128], tl, NT))
            F[i // 4, i % 4, x] = f[:, 0:128]
            F[i // 4, i % 4, x + 1] = f[:, 128:256]
        if send_now:
            core_copy(me, F, RD, dsem, i).start()

    def factor_loop(lo, hi, send_now):
        def body(i, _):
            factors(i, send_now)
            return 0
        lax.fori_loop(lo, hi, body, 0)
    factor_loop(0, 4, False)
    for c in fcopy:
        c.wait()
    for h in range(2):
        ftr[h] = fbuf[h].T
    for k in range(8):
        m8[k:k + 1, :] = mix[k:k + 1, :] * math.exp(-float(k * k))
    for p in range(4):
        own_positions(H, PI, p)
    greeted()
    for i in range(4):
        core_copy(me, F, RD, dsem, i).start()
    cp = Copies(send, recv)
    hs = halo_steps(me, cp, H)
    hs[0]()

    def filt(h):
        return lambda: ftr[h, pl.ds(pl.multiple_of(me.core * 64 + 8 * me.z, 8), 8), :] * FILTER_SCALE

    rs = [reduce_steps(me, cp, F, G, (RD, R1, R2, R3, RZ), dsem, filt(h), h) for h in range(2)]

    def convert(dst, at_of, cells_of, n):
        def body(i, _):
            make_vb(H, dst, at_of(i), *cells_of(i))
            return 0
        lax.fori_loop(0, n, body, 0)

    def potential(h):
        def body(j, acc):
            y, t = j // 2, j % 2
            g = jnp.concatenate([G[h, y, 2 * t], G[h, y, 2 * t + 1]], axis=1)
            gh, gl = split(g)
            k = 4 * h + y + 8 * t
            big = mm(jnp.concatenate([gh, gl], axis=0), TH[k], NN)
            return acc + (big[0:128] + (big[128:256] + mm(gh, TL[k], NN)))
        potr[...] = lax.fori_loop(0, 8, body, potr[...] if h else jnp.zeros((128, 512), f32))

    at = [0, 0, 0, 0]
    for item in PLAN:
        if item[0] == "h":
            hs[item[1]]()
        elif item[0] == "r":
            rs[item[1]][item[2]]()
        elif item[0] == "factors":
            factor_loop(item[1], item[2], True)
        elif item[0] == "pot":
            potential(item[1])
        elif item[0] == "ca":
            for n in range(4):
                make_vb(H, va, (n,), *OWN_CELLS[n])
        elif item[0] == "cA":
            for n in range(4, 12):
                make_vb(H, va, (n,), *OWN_CELLS[n])
        elif item[0] == "cB":
            convert(vy, lambda i: (i // 6, (i // 3) % 2, i % 3), lambda i: (1 + (i // 3) % 2, 3 * (i // 6), i % 3), 12)
        elif item[0] == "cC":
            convert(vb, lambda i: (i // 12, (i // 3) % 4, i % 3), lambda i: (3 * (i // 12), (i // 3) % 4, i % 3), 24)
        else:
            def body(t, _, phase=item[0]):
                pair_unit(H, PI, va, vy, vb, K, m8, msg, t, phase)
                return 0
            lax.fori_loop(at[item[0]], at[item[0]] + item[1], body, 0)
            at[item[0]] += item[1]

    for p, c in enumerate(cells):
        mixed = feat[c] + 0.125 * msg[p].T + potr[:, p * 128:(p + 1) * 128]
        h = mm3(wh[...], mixed, TN)
        h = h / (1.0 + jnp.exp(-h))
        o = mixed + mm3(wo[...], h, TN)
        out[c] = jnp.where(lane < counts[c[0], 0, c[1]], o, 0.0)
    cp.finish()
    for i in range(8):
        core_copy(me, F, RD, dsem, i).wait_send()


NCOPY = 176


def shards(features, positions, counts, waves, filter_table, w_value, w_charge, radial_mix, w_hidden, w_out):
    V = pl.BlockSpec(memory_space=pltpu.VMEM)
    S = pl.BlockSpec(memory_space=pltpu.SMEM)
    A = pl.BlockSpec(memory_space=pl.ANY)
    vm = pltpu.VMEM
    return pl.pallas_call(
        kernel,
        out_shape=jax.ShapeDtypeStruct(features.shape, f32),
        in_specs=[V, V, S, V, A, V, V, V, V, V], out_specs=V,
        scratch_shapes=[
            vm((4, 4, 3, 136, 128), f32), vm((2, 4, 4, 128, 128), f32), vm((2, 4, 4, 128, 128), f32),
            vm((2, 4, 4, 64, 128), f32), vm((2, 4, 2, 4, 16, 128), f32),
            vm((2, 4, 4, 16, 128), f32), vm((2, 4, 3, 16, 128), f32),
            vm((2, 8, 8, 128), f32),
            vm((16, 256, 512), bf16), vm((16, 256, 512), bf16), vm((256, 512), bf16), vm((16, 2048), bf16),
            vm((2, 128, 128), f32), vm((2, 128, 128), f32),
            vm((12, 128, 256), bf16), vm((2, 2, 3, 128, 256), bf16), vm((2, 4, 3, 128, 256), bf16), vm((4, 3, 128, 128), f32),
            vm((16 * IC, 1152), bf16), vm((8, 128), f32), vm((4, 128, 128), f32), vm((128, 512), f32),
            pltpu.SemaphoreType.DMA((NCOPY,)), pltpu.SemaphoreType.DMA((NCOPY,)),
            pltpu.SemaphoreType.DMA((2, 8)), pltpu.SemaphoreType.DMA((2,)),
        ],
        compiler_params=pltpu.CompilerParams(collective_id=0, has_side_effects=True),
        name="layer",
    )(features, positions.reshape(2, 2, 3, 1, 128), counts.reshape(2, 1, 2), waves, filter_table,
      w_value, w_charge, radial_mix, w_hidden, w_out)


def solution(mesh):
    cell = P("gx", "gy", "gz")
    five = P("gx", "gy", "gz", None, None)
    return jax.shard_map(
        shards, mesh=mesh,
        in_specs=(five, five, cell) + (P(),) * 7,
        out_specs=five, check_vma=False)
```
